256 devices in a mesh: batch: 16 (over x, y_hi, core), space: 16 (over z, y_lo).
Axes of the slice: x: 4, y: 4 (y_hi: 2, y_lo: 2; y = y_hi * 2 + y_lo), z: 8, core: 2. Of those that a mesh axis runs over, the one named last changes fastest.
Arguments:
- snapshots: bfloat16 [16, 64, 32, 1024], P('batch', None, 'space'), may hold values from -6 to 6
- cotangent: bfloat16 [16, 64, 32, 1024], P('batch', None, 'space'), may hold values from -6 to 6
- mode_weight: bfloat16 [16, 16, 24, 64, 64], P('batch', 'space'), may hold values from -0.75 to 0.75
- conv_weight: bfloat16 [3, 3, 3, 64, 64], replicated, may hold values from -0.15625 to 0.15625
Outputs:
- activated: bfloat16 [16, 64, 32, 1024], P('batch', None, 'space')
- input_gradient: bfloat16 [16, 64, 32, 1024], P('batch', None, 'space')
- mode_gradient: float32 [16, 16, 24, 64, 64], P('batch', 'space')
- conv_gradient: float32 [3, 3, 3, 64, 64], replicated
The draws below stay inside these ranges and needn't reach their ends.
All inputs are finite; a program needn't handle non-finite values.
Results may differ from the reference program's by a relative error of at most 0.02.
Values may be sent and summed in bfloat16 or wider, within the bound.
A program may use at most 128 MiB of HBM per device.

```python
import math
import jax
import jax.numpy as jnp
from jax import lax

C = 64
KX = 8
KY = 8
KZ = 12
NX = 32
NY = 32
PX = 16
PY = 16
PZ = 24
NZ = 32
PLANE = 1024
SNAPS = 16


def shard_levels(rng, dims, cuts, least, top_value):
    loudness, own = 1.0, jax.random.fold_in(rng, 6)
    for axis_at, parts in cuts:
        steps = jnp.exp(jax.random.uniform(jax.random.fold_in(own, axis_at), (parts,), jnp.float32, least / len(cuts), top_value / len(cuts)))
        loudness = loudness * jnp.repeat(steps, dims[axis_at] // parts).reshape([-1 if axis == axis_at else 1 for axis in range(len(dims))])
    return loudness


def gaussian(stream_key, extent, scale, most, cuts=(), kind=jnp.bfloat16):
    result = jax.random.normal(stream_key, extent, jnp.float32) * scale
    if len(cuts) > 0:
        result = shard_levels(stream_key, extent, cuts, -0.22, 0.18) * result
    return jnp.clip(result, min=-most, max=most).astype(kind)


def setup_inputs(seed: int = 0) -> dict:
    arg_keys = jax.random.split(jax.random.key(seed), 5)
    snapshots = gaussian(arg_keys[0], (SNAPS, C, NZ, PLANE), 1.0, 6.0, ((0, 16), (2, 16)))
    cotangent = gaussian(arg_keys[1], (SNAPS, C, NZ, PLANE), 1.0, 6.0, ((0, 16), (2, 16)))
    mode_weight = gaussian(arg_keys[2], (PX, PY, PZ, C, C), C ** -0.5, 0.75, ((0, 16), (1, 16)))
    conv_weight = gaussian(arg_keys[3], (3, 3, 3, C, C), (27 * C) ** -0.5, 0.15625)
    return dict(snapshots=snapshots, cotangent=cotangent, mode_weight=mode_weight, conv_weight=conv_weight)


inv_root_two = 1.0 / math.sqrt(2.0)
inv_root_two_pi = 1.0 / math.sqrt(2.0 * math.pi)

def basis_rows(half_count, length):
    row_index = lax.broadcasted_iota(jnp.int32, (2 * half_count, length), 0)
    cell_index = lax.broadcasted_iota(jnp.int32, (2 * half_count, length), 1)
    frequency = jnp.where(row_index < half_count, row_index, row_index - half_count + 1)
    phases = (frequency * cell_index % length).astype(jnp.float32) * (2.0 * math.pi / length)
    return jnp.where(row_index < half_count, jnp.cos(phases), jnp.sin(phases))

def make_tables(count_x, count_y, count_z, length_x, length_y, length_z):
    across = basis_rows(count_x, length_x)
    along_y = basis_rows(count_y, length_y)
    depth_rows = basis_rows(count_z, length_z)
    modes_x = 2 * count_x
    modes_y = 2 * count_y
    outer_table = (across[:, None, :, None] * along_y[None, :, None, :]).reshape(modes_x * modes_y, length_x * length_y)
    plane_analysis = (outer_table * (2.0 / math.sqrt(length_x * length_y))).astype(jnp.bfloat16)
    plane_synthesis = (outer_table.T * (2.0 / math.sqrt(modes_x * modes_y))).astype(jnp.bfloat16)
    depth_analysis = (depth_rows * math.sqrt(2.0 / length_z)).astype(jnp.bfloat16)
    depth_synthesis = (depth_rows.T * math.sqrt(2.0 / (2 * count_z))).astype(jnp.bfloat16)
    return (plane_analysis, plane_synthesis, depth_analysis, depth_synthesis)

def highest_einsum(formula, left, right):
    return jnp.einsum(formula, left.astype(jnp.float32), right.astype(jnp.float32), precision=lax.Precision.HIGHEST)

def stencil(padded, kernel):
    channels = padded.shape[0]
    depth_cells = padded.shape[1] - 2
    summed = jnp.zeros((kernel.shape[4], depth_cells * NX * NY), jnp.float32)
    for offset_x in range(3):
        for offset_y in range(3):
            window = padded[:, :, offset_x:offset_x + NX, offset_y:offset_y + NY]
            stacked = jnp.stack([window[:, offset_z:offset_z + depth_cells] for offset_z in range(3)], 0)
            stacked = stacked.reshape(3, channels, depth_cells * NX * NY).astype(jnp.float32)
            summed = summed + lax.dot_general(kernel[:, offset_x, offset_y].astype(jnp.float32), stacked, (((0, 1), (0, 1)), ((), ())), precision=lax.Precision.HIGHEST)
    return summed

def kernel_terms(padded, pre_flat):
    channels = padded.shape[0]
    depth_cells = padded.shape[1] - 2
    pieces = []
    for offset_x in range(3):
        row_pieces = []
        for offset_y in range(3):
            window = padded[:, :, offset_x:offset_x + NX, offset_y:offset_y + NY]
            stacked = jnp.stack([window[:, offset_z:offset_z + depth_cells] for offset_z in range(3)], 0)
            stacked = stacked.reshape(3, channels, depth_cells * NX * NY).astype(jnp.float32)
            row_pieces.append(lax.dot_general(stacked, pre_flat.astype(jnp.float32), (((2,), (1,)), ((), ())), precision=lax.Precision.HIGHEST))
        pieces.append(jnp.stack(row_pieces, 1))
    return jnp.stack(pieces, 1)

def widen(field):
    channels, depth_cells, plane = field.shape
    return jnp.pad(field.reshape(channels, depth_cells, NX, NY), ((0, 0), (1, 1), (1, 1), (1, 1)))

def one_snapshot(tables, mode_weight, conv_weight, snapshot, cotangent):
    plane_analysis, plane_synthesis, depth_analysis, depth_synthesis = tables
    channels, depth_len, plane = snapshot.shape
    modes_x = 2 * KX
    modes_y = 2 * KY
    plane_coef = lax.dot_general(snapshot.reshape(channels * depth_len, plane), plane_analysis, (((1,), (1,)), ((), ())), preferred_element_type=jnp.float32)
    plane_coef = plane_coef.astype(jnp.bfloat16).reshape(channels, depth_len, modes_x, modes_y)
    coef = highest_einsum('czxy,pz->cpxy', plane_coef, depth_analysis).astype(jnp.bfloat16)
    mixed = highest_einsum('ipxy,xypio->opxy', coef, mode_weight).astype(jnp.bfloat16)
    depth_back = highest_einsum('opxy,zp->ozxy', mixed, depth_synthesis).astype(jnp.bfloat16)
    spectral = lax.dot_general(depth_back.reshape(channels * depth_len, modes_x * modes_y), plane_synthesis, (((1,), (1,)), ((), ())), preferred_element_type=jnp.float32)
    padded = widen(snapshot)
    pre = spectral.reshape(channels, depth_len * plane) + stencil(padded, conv_weight)
    normal_cdf = 0.5 * (1.0 + lax.erf(pre * inv_root_two))
    density = jnp.exp(-0.5 * pre * pre) * inv_root_two_pi
    activated = (pre * normal_cdf).astype(jnp.bfloat16).reshape(channels, depth_len, plane)
    pre_grad = (cotangent.reshape(channels, depth_len * plane).astype(jnp.float32) * (normal_cdf + pre * density)).astype(jnp.bfloat16)
    back_plane = jnp.dot(pre_grad.reshape(channels * depth_len, plane), plane_synthesis, preferred_element_type=jnp.float32)
    back_plane = back_plane.astype(jnp.bfloat16).reshape(channels, depth_len, modes_x, modes_y)
    mixed_grad = highest_einsum('ozxy,zp->opxy', back_plane, depth_synthesis).astype(jnp.bfloat16)
    weight_term = highest_einsum('ipxy,opxy->xypio', coef, mixed_grad)
    coef_grad = highest_einsum('opxy,xypio->ipxy', mixed_grad, mode_weight).astype(jnp.bfloat16)
    depth_grad = highest_einsum('ipxy,pz->izxy', coef_grad, depth_analysis).astype(jnp.bfloat16)
    spectral_grad = jnp.dot(depth_grad.reshape(channels * depth_len, modes_x * modes_y), plane_analysis, preferred_element_type=jnp.float32)
    flipped = jnp.transpose(conv_weight[::-1, ::-1, ::-1], (0, 1, 2, 4, 3))
    local_grad = stencil(widen(pre_grad.reshape(channels, depth_len, plane)), flipped)
    input_gradient = (spectral_grad.reshape(channels, depth_len * plane) + local_grad).astype(jnp.bfloat16).reshape(channels, depth_len, plane)
    kernel_term = kernel_terms(padded, pre_grad)
    return (activated, input_gradient, weight_term, kernel_term)

def reference(snapshots, cotangent, mode_weight, conv_weight):
    tables = make_tables(KX, KY, KZ, NX, NY, NZ)

    def advance(carry, inputs):
        weight_sum, kernel_sum = carry
        activated, input_gradient, weight_term, kernel_term = one_snapshot(tables, mode_weight, conv_weight, inputs[0], inputs[1])
        return ((weight_sum + weight_term, kernel_sum + kernel_term), (activated, input_gradient))
    start_sums = (jnp.zeros(mode_weight.shape, jnp.float32), jnp.zeros(conv_weight.shape, jnp.float32))
    (mode_gradient, kernel_sum), (activated, input_gradient) = lax.scan(advance, start_sums, (snapshots, cotangent))
    conv_gradient = kernel_sum / math.sqrt(SNAPS * NZ * PLANE)
    return (activated, input_gradient, mode_gradient, conv_gradient)
```

```python
import math

import jax
import jax.numpy as jnp
import ml_dtypes
import numpy as np
from jax import lax
from jax.experimental import pallas as pl
from jax.experimental.pallas import tpu as pltpu
from jax.sharding import PartitionSpec as P

KX = 8
KY = 8
KZ = 12
NX = 32
NY = 32
NZ = 32
PLANE = NX * NY
C = 64
G = 16
SNAPS = 16

MESH = pl.DeviceIdType.MESH
F32 = jnp.float32
BF16 = jnp.bfloat16

inv_root_two = 1.0 / math.sqrt(2.0)
inv_root_two_pi = 1.0 / math.sqrt(2.0 * math.pi)
conv_scale = 1.0 / math.sqrt(SNAPS * NZ * PLANE)


def basis_rows(half_count, length):
    rows = np.arange(2 * half_count)[:, None]
    cells = np.arange(length)[None, :]
    frequency = np.where(rows < half_count, rows, rows - half_count + 1)
    phases = ((frequency * cells) % length).astype(np.float32) * np.float32(2.0 * math.pi / length)
    return np.where(rows < half_count, np.cos(phases), np.sin(phases)).astype(np.float32)


def make_tables():
    across = basis_rows(KX, NX)
    along_y = basis_rows(KY, NY)
    depth_rows = basis_rows(KZ, NZ)
    outer = across[None, :, :, None] * along_y[:, None, None, :]
    plane = (outer.reshape(256, PLANE) * np.float32(2.0 / math.sqrt(PLANE))).astype(ml_dtypes.bfloat16)
    analysis = (depth_rows * np.float32(math.sqrt(2.0 / NZ))).astype(ml_dtypes.bfloat16)
    synthesis = (depth_rows.T * np.float32(math.sqrt(2.0 / (2 * KZ)))).astype(ml_dtypes.bfloat16)
    to_modes = np.zeros((2, G, 16, 2, G, 16), ml_dtypes.bfloat16)
    to_cells = np.zeros((2, G, 16, 2, G, 16), ml_dtypes.bfloat16)
    down = analysis.reshape(2, KZ, 16, 2).transpose(0, 1, 3, 2)
    up = synthesis.reshape(16, 2, 2, KZ).transpose(1, 0, 2, 3)
    for mode in range(16):
        to_modes[:, mode, :KZ, :, :, mode] = down
        to_cells[:, :, mode, :, mode, :KZ] = up
    to_modes = to_modes.reshape(512, 512)
    to_cells = to_cells.reshape(512, 512)
    depth = np.stack([to_modes, to_cells, to_cells.T, to_modes.T])
    swap = np.zeros((16, 16, 16, 16), ml_dtypes.bfloat16)
    for a in range(16):
        for b in range(16):
            swap[a, b, b, a] = 1
    x = np.arange(PLANE) // NY
    y = np.arange(PLANE) % NY
    inside = np.zeros((16, PLANE), ml_dtypes.bfloat16)
    for tap in range(9):
        dx, dy = tap // 3 - 1, tap % 3 - 1
        inside[tap] = (x + dx >= 0) & (x + dx < NX) & (y + dy >= 0) & (y + dy < NY)
    return plane, depth, swap.reshape(256, 256), inside


def mm(left, right, left_dim=1, right_dim=0):
    return lax.dot_general(
        left, right, (((left_dim,), (right_dim,)), ((), ())), preferred_element_type=F32
    )


def kernel(
    x_in, cot_in, w_in, cw_in, plane_in, depth_in, swap_in, inside_in,
    act_out, grad_out, mode_out, conv_out,
    x, cot, w, cw, plane, depth, swap, inside,
    act, grad, mode, conv,
    send, recv, halo, pre_halo, cols, forward_w, back_w, mix_w, total, pg, coef, coef_back,
    part_send, part_recv, term_send, term_recv, full_send, full_recv,
    in_sem, out_sem, send_sem, recv_sem, halo_sem, sum_send_sem, sum_recv_sem,
):
    me_b = lax.axis_index("batch")
    me_s = lax.axis_index("space")
    mine = {"batch": me_b, "space": me_s}

    loads = [
        pltpu.make_async_copy(source, target, in_sem.at[i])
        for i, (source, target) in enumerate(
            (
                (x_in, x), (plane_in, plane), (depth_in, depth), (inside_in, inside),
                (cw_in, cw), (swap_in, swap), (w_in, w), (cot_in, cot),
            )
        )
    ]
    for load in loads:
        load.start()

    barrier = pltpu.get_barrier_semaphore()

    def greet(step, carry):
        for axis in ("space", "batch"):
            peer = lax.rem(mine[axis] + step, G)
            pl.semaphore_signal(barrier, inc=1, device_id={axis: peer}, device_id_type=MESH)
        return carry

    lax.fori_loop(1, G, greet, 0)

    def tile_copy(phase, axis, source, slot):
        return pltpu.make_async_remote_copy(
            src_ref=send.at[phase, source],
            dst_ref=recv.at[phase, slot],
            send_sem=send_sem.at[phase, source],
            recv_sem=recv_sem.at[phase, slot],
            device_id={axis: source},
            device_id_type=MESH,
        )

    def exchange_start(phase, axis, value):
        me = mine[axis]
        send[phase] = value.reshape(G, 16, 128)
        recv[phase, me] = send[phase, me]

        def step(i, carry):
            tile_copy(phase, axis, lax.rem(me + i, G), me).start()
            return carry

        lax.fori_loop(1, G, step, 0)

    def exchange_wait(phase, axis):
        me = mine[axis]

        def step(i, carry):
            peer = lax.rem(me + i, G)
            tile_copy(phase, axis, peer, peer).wait_recv()
            return carry

        lax.fori_loop(1, G, step, 0)
        return recv[phase].reshape(256, 128)

    def exchange_drain(phase, axis):
        me = mine[axis]

        def step(i, carry):
            tile_copy(phase, axis, lax.rem(me + i, G), me).wait_send()
            return carry

        lax.fori_loop(1, G, step, 0)

    def halo_copy(source, target, slot, which, offset):
        return pltpu.make_async_remote_copy(
            src_ref=source,
            dst_ref=target.at[slot],
            send_sem=halo_sem.at[0, which],
            recv_sem=halo_sem.at[1, which],
            device_id={"space": lax.rem(me_s + offset, G)},
            device_id_type=MESH,
        )

    def depth_transform(which, tiles):
        stacked = jnp.concatenate([tiles[:, :C], tiles[:, C:]], axis=0)
        both = mm(depth[which], stacked)
        return jnp.concatenate([both[:256], both[256:]], axis=1).astype(BF16)

    def spread(layer, cells):
        for tap in range(9):
            shift = (tap // 3 - 1) * NY + (tap % 3 - 1)
            moved = cells
            if shift:
                moved = pltpu.roll(cells, (-shift) % PLANE, 1) * inside[tap : tap + 1, :]
            cols[tap * C : (tap + 1) * C, layer * PLANE : (layer + 1) * PLANE] = moved

    def stencil(weights):
        width = 256
        for chunk in range(PLANE // width):
            lanes = [pl.ds(layer * PLANE + chunk * width, width) for layer in range(4)]
            acc = mm(weights[C : 3 * C, :], cols[:, lanes[1]])
            acc = acc + mm(weights[0 : 2 * C, :], cols[:, lanes[2]])
            first = mm(weights[2 * C : 3 * C, :], cols[:, lanes[0]])
            last = mm(weights[0:C, :], cols[:, lanes[3]])
            total[:, pl.ds(chunk * width, width)] = acc + jnp.concatenate([first, last], axis=0)

    loads[0].wait()
    loads[1].wait()
    both_layers = jnp.concatenate([x[:, :PLANE], x[:, PLANE:]], axis=0)
    plane_coef = mm(plane[...], both_layers, 1, 1).astype(BF16)
    pl.semaphore_wait(barrier, 2 * (G - 1))
    exchange_start(0, "space", plane_coef)
    halos = [
        halo_copy(x.at[:, pl.ds(PLANE, PLANE)], halo, 0, 0, 1),
        halo_copy(x.at[:, pl.ds(0, PLANE)], halo, 1, 1, G - 1),
    ]
    for copy in halos:
        copy.start()

    loads[2].wait()
    loads[3].wait()
    spread(1, x[:, :PLANE])
    tiles = exchange_wait(0, "space")
    exchange_start(1, "batch", depth_transform(0, tiles))

    loads[4].wait()
    for a in range(3):
        for tap in range(9):
            block = cw[a, tap]
            forward_w[(2 - a) * C : (3 - a) * C, tap * C : (tap + 1) * C] = (
                block.astype(F32).T.astype(BF16)
            )
            back_w[a * C : (a + 1) * C, (8 - tap) * C : (9 - tap) * C] = block
    loads[5].wait()
    loads[6].wait()
    mix_w[...] = jnp.zeros_like(mix_w)
    for p in range(KZ):
        mix_w[p, :C, :C] = w[p]
        mix_w[p, C:, C:] = w[KZ + p]

    tiles = exchange_wait(1, "batch")
    coef[...] = mm(swap[...], tiles).astype(BF16)

    def rows_of(p):
        return pl.ds(p * 16, 16)

    def pad_and_swap(pieces):
        value = jnp.concatenate(pieces + [jnp.zeros((64, 128), F32)], axis=0).astype(BF16)
        return mm(swap[...], value).astype(BF16)

    mixed = [mm(coef[rows_of(p), :], mix_w[p]) for p in range(KZ)]
    exchange_start(2, "batch", pad_and_swap(mixed))

    spread(2, x[:, PLANE:])
    for copy in halos:
        copy.wait_recv()
    spread(0, jnp.where(me_s > 0, halo[0], jnp.zeros_like(halo[0])))
    spread(3, jnp.where(me_s < G - 1, halo[1], jnp.zeros_like(halo[1])))

    tiles = exchange_wait(2, "batch")
    exchange_start(3, "space", depth_transform(1, tiles))
    stencil(forward_w)
    loads[7].wait()
    tiles = exchange_wait(3, "space")
    doubled = tiles * jnp.asarray(2.0, BF16)

    for chunk in range(4):
        lanes = pl.ds(chunk * 256, 256)
        total[:, lanes] += mm(doubled, plane[:, lanes], 0, 0)
    for layer in range(2):
        for chunk in range(4):
            lanes = pl.ds(chunk * 256, 256)
            cells = pl.ds(layer * PLANE + chunk * 256, 256)
            rows = pl.ds(layer * C, C)
            pre = total[rows, lanes]
            normal_cdf = 0.5 * (1.0 + lax.erf(pre * inv_root_two))
            density = jnp.exp(-0.5 * pre * pre) * inv_root_two_pi
            act[:, cells] = (pre * normal_cdf).astype(BF16)
            pg[rows, lanes] = (
                cot[:, cells].astype(F32) * (normal_cdf + pre * density)
            ).astype(BF16)
    stores = [pltpu.make_async_copy(act, act_out, out_sem.at[0])]
    stores[0].start()

    back_plane = (mm(plane[...], pg[...], 1, 1) * 2.0).astype(BF16)
    exchange_start(4, "space", back_plane)
    pre_halos = [
        halo_copy(pg.at[pl.ds(C, C), :], pre_halo, 0, 2, 1),
        halo_copy(pg.at[pl.ds(0, C), :], pre_halo, 1, 3, G - 1),
    ]
    for copy in pre_halos:
        copy.start()

    for r in range(3):
        rows = pl.ds(r * 192, 192)
        by_layer = [
            mm(cols[rows, pl.ds(layer * PLANE, PLANE)], pg[...], 1, 1) for layer in range(4)
        ]
        terms = [by_layer[a][:, :C] + by_layer[a + 1][:, C:] for a in range(3)]
        part_send[rows, :] = jnp.concatenate(terms[:2], axis=1).astype(BF16)
        part_send[pl.ds(576 + r * 96, 96), :] = jnp.concatenate(
            [terms[2][:96], terms[2][96:]], axis=1
        ).astype(BF16)
    part_send[pl.ds(864, 160), :] = jnp.zeros((160, 128), BF16)

    def sum_copy(stage, axis, source, target, peer, slot):
        return pltpu.make_async_remote_copy(
            src_ref=source,
            dst_ref=target.at[slot],
            send_sem=sum_send_sem.at[stage, peer],
            recv_sem=sum_recv_sem.at[stage, slot],
            device_id={axis: peer},
            device_id_type=MESH,
        )

    def part_rows(i):
        return part_send.at[pl.ds(pl.multiple_of(i * 64, 64), 64), :]

    stages = (
        ("space", part_rows, part_recv),
        ("batch", lambda i: term_send, term_recv),
        ("space", lambda i: full_send, full_recv),
    )

    def sum_start(stage):
        axis, source, target = stages[stage]
        me = mine[axis]
        target[me] = source(me)[...]

        def step(i, carry):
            peer = lax.rem(me + i, G)
            sum_copy(stage, axis, source(peer), target, peer, me).start()
            return carry

        lax.fori_loop(1, G, step, 0)

    def sum_wait(stage):
        axis, source, target = stages[stage]
        me = mine[axis]

        def step(i, carry):
            peer = lax.rem(me + i, G)
            sum_copy(stage, axis, source(peer), target, peer, peer).wait_recv()
            return carry

        lax.fori_loop(1, G, step, 0)

    def sum_drain(stage):
        axis, source, target = stages[stage]
        me = mine[axis]

        def step(i, carry):
            peer = lax.rem(me + i, G)
            sum_copy(stage, axis, source(peer), target, peer, me).wait_send()
            return carry

        lax.fori_loop(1, G, step, 0)

    def added(target):
        value = target[0].astype(F32)
        for i in range(1, G):
            value = value + target[i].astype(F32)
        return value

    tiles = exchange_wait(4, "space")
    exchange_start(5, "batch", depth_transform(2, tiles))
    sum_start(0)

    spread(1, pg[:C, :])
    tiles = exchange_wait(5, "batch")
    coef_back[...] = mm(swap[...], tiles).astype(BF16)
    gradients = [mm(coef_back[rows_of(p), :], mix_w[p], 1, 1) for p in range(KZ)]
    exchange_start(6, "batch", pad_and_swap(gradients))

    for p in range(KZ):
        product = mm(coef[rows_of(p), :], coef_back[rows_of(p), :], 0, 0)
        mode[p] = product[:C, :C]
        mode[KZ + p] = product[C:, C:]
    stores.append(pltpu.make_async_copy(mode, mode_out, out_sem.at[1]))
    stores[1].start()

    spread(2, pg[C:, :])
    sum_wait(0)
    term_send[...] = added(part_recv).astype(BF16)
    sum_start(1)

    tiles = exchange_wait(6, "batch")
    exchange_start(7, "space", depth_transform(3, tiles))

    for copy in pre_halos:
        copy.wait_recv()
    spread(0, jnp.where(me_s > 0, pre_halo[0], jnp.zeros_like(pre_halo[0])))
    spread(3, jnp.where(me_s < G - 1, pre_halo[1], jnp.zeros_like(pre_halo[1])))
    sum_wait(1)
    full_send[...] = (added(term_recv) * conv_scale).astype(BF16)
    sum_start(2)
    stencil(back_w)

    tiles = exchange_wait(7, "space")
    for chunk in range(4):
        lanes = pl.ds(chunk * 256, 256)
        value = (total[:, lanes] + mm(tiles, plane[:, lanes], 0, 0)).astype(BF16)
        grad[:, lanes] = value[:C]
        grad[:, pl.ds(PLANE + chunk * 256, 256)] = value[C:]
    stores.append(pltpu.make_async_copy(grad, grad_out, out_sem.at[2]))
    stores[2].start()

    sum_wait(2)
    for i in range(9):
        value = full_recv[i].astype(F32)
        conv[pl.ds(i * 64, 64), :] = value[:, :C]
        conv[pl.ds(576 + i * 64, 64), :] = value[:, C:]
    rest = full_recv[9:14].reshape(320, 128).astype(F32)
    for r in range(3):
        conv[pl.ds(1152 + r * 192, 96), :] = rest[r * 96 : (r + 1) * 96, :C]
        conv[pl.ds(1152 + r * 192 + 96, 96), :] = rest[r * 96 : (r + 1) * 96, C:]
    stores.append(pltpu.make_async_copy(conv, conv_out, out_sem.at[3]))
    stores[3].start()

    for phase, axis in enumerate(("space", "batch", "batch", "space") * 2):
        exchange_drain(phase, axis)
    for stage in range(3):
        sum_drain(stage)
    for copy in halos + pre_halos:
        copy.wait_send()
    for store in stores:
        store.wait()


def shards(snapshots, cotangent, mode_weight, conv_weight):
    plane, depth, swap, inside = make_tables()
    any_space = pl.BlockSpec(memory_space=pl.ANY)
    vmem = pltpu.VMEM
    dma = pltpu.SemaphoreType.DMA
    outs = pl.pallas_call(
        kernel,
        name="layer",
        out_shape=(
            jax.ShapeDtypeStruct((C, 2 * PLANE), BF16),
            jax.ShapeDtypeStruct((C, 2 * PLANE), BF16),
            jax.ShapeDtypeStruct((2 * KZ, C, C), F32),
            jax.ShapeDtypeStruct((27 * C, C), F32),
        ),
        in_specs=[any_space] * 8,
        out_specs=(any_space,) * 4,
        scratch_shapes=[
            vmem((C, 2 * PLANE), BF16),
            vmem((C, 2 * PLANE), BF16),
            vmem((2 * KZ, C, C), BF16),
            vmem((3, 9, C, C), BF16),
            vmem((256, PLANE), BF16),
            vmem((4, 512, 512), BF16),
            vmem((256, 256), BF16),
            vmem((16, PLANE), BF16),
            vmem((C, 2 * PLANE), BF16),
            vmem((C, 2 * PLANE), BF16),
            vmem((2 * KZ, C, C), F32),
            vmem((27 * C, C), F32),
            vmem((8, G, 16, 128), BF16),
            vmem((8, G, 16, 128), BF16),
            vmem((2, C, PLANE), BF16),
            vmem((2, C, PLANE), BF16),
            vmem((9 * C, 4 * PLANE), BF16),
            vmem((3 * C, 9 * C), BF16),
            vmem((3 * C, 9 * C), BF16),
            vmem((KZ, 128, 128), BF16),
            vmem((128, PLANE), F32),
            vmem((128, PLANE), BF16),
            vmem((256, 128), BF16),
            vmem((256, 128), BF16),
            vmem((1024, 128), BF16),
            vmem((G, 64, 128), BF16),
            vmem((64, 128), BF16),
            vmem((G, 64, 128), BF16),
            vmem((64, 128), BF16),
            vmem((G, 64, 128), BF16),
            dma((8,)),
            dma((4,)),
            dma((8, G)),
            dma((8, G)),
            dma((2, 4)),
            dma((3, G)),
            dma((3, G)),
        ],
        compiler_params=pltpu.CompilerParams(
            collective_id=0, has_side_effects=True, vmem_limit_bytes=40 << 20
        ),
    )(
        snapshots.reshape(C, 2 * PLANE),
        cotangent.reshape(C, 2 * PLANE),
        mode_weight.reshape(2 * KZ, C, C),
        conv_weight.reshape(3, 9, C, C),
        jnp.asarray(plane),
        jnp.asarray(depth),
        jnp.asarray(swap),
        jnp.asarray(inside),
    )
    activated, input_gradient, mode_gradient, conv_gradient = outs
    return (
        activated.reshape(1, C, 2, PLANE),
        input_gradient.reshape(1, C, 2, PLANE),
        mode_gradient.reshape(1, 1, 2 * KZ, C, C),
        conv_gradient.reshape(3, 3, 3, C, C),
    )


def solution(mesh):
    in_specs = (
        P("batch", None, "space", None),
        P("batch", None, "space", None),
        P("batch", "space", None, None, None),
        P(),
    )
    out_specs = in_specs
    return jax.shard_map(shards, mesh=mesh, in_specs=in_specs, out_specs=out_specs, check_vma=False)
```

```python
import math

import jax
import jax.numpy as jnp
import ml_dtypes
import numpy as np
from jax import lax
from jax.experimental import pallas as pl
from jax.experimental.pallas import tpu as pltpu
from jax.sharding import PartitionSpec as P

KX = 8
KY = 8
KZ = 12
NX = 32
NY = 32
NZ = 32
PLANE = NX * NY
C = 64
G = 16
SNAPS = 16

MESH = pl.DeviceIdType.MESH
F32 = jnp.float32
BF16 = jnp.bfloat16

inv_root_two = 1.0 / math.sqrt(2.0)
inv_root_two_pi = 1.0 / math.sqrt(2.0 * math.pi)
conv_scale = 1.0 / math.sqrt(SNAPS * NZ * PLANE)


def basis_rows(half_count, length):
    rows = np.arange(2 * half_count)[:, None]
    cells = np.arange(length)[None, :]
    frequency = np.where(rows < half_count, rows, rows - half_count + 1)
    phases = ((frequency * cells) % length).astype(np.float32) * np.float32(2.0 * math.pi / length)
    return np.where(rows < half_count, np.cos(phases), np.sin(phases)).astype(np.float32)


def make_tables():
    across = basis_rows(KX, NX)
    along_y = basis_rows(KY, NY)
    depth_rows = basis_rows(KZ, NZ)
    outer = across[None, :, :, None] * along_y[:, None, None, :]
    plane = (outer.reshape(256, PLANE) * np.float32(2.0 / math.sqrt(PLANE))).astype(ml_dtypes.bfloat16)
    analysis = (depth_rows * np.float32(math.sqrt(2.0 / NZ))).astype(ml_dtypes.bfloat16)
    synthesis = (depth_rows.T * np.float32(math.sqrt(2.0 / (2 * KZ)))).astype(ml_dtypes.bfloat16)
    to_modes = np.zeros((2, G, 16, 2, G, 16), ml_dtypes.bfloat16)
    to_cells = np.zeros((2, G, 16, 2, G, 16), ml_dtypes.bfloat16)
    down = analysis.reshape(2, KZ, 16, 2).transpose(0, 1, 3, 2)
    up = synthesis.reshape(16, 2, 2, KZ).transpose(1, 0, 2, 3)
    for mode in range(16):
        to_modes[:, mode, :KZ, :, :, mode] = down
        to_cells[:, :, mode, :, mode, :KZ] = up
    to_modes = to_modes.reshape(512, 512)
    to_cells = to_cells.reshape(512, 512)
    depth = np.stack([to_modes, to_cells, to_cells.T, to_modes.T])
    swap = np.zeros((16, 16, 16, 16), ml_dtypes.bfloat16)
    for a in range(16):
        for b in range(16):
            swap[a, b, b, a] = 1
    x = np.arange(PLANE) // NY
    y = np.arange(PLANE) % NY
    inside = np.zeros((16, PLANE), ml_dtypes.bfloat16)
    for tap in range(9):
        dx, dy = tap // 3 - 1, tap % 3 - 1
        inside[tap] = (x + dx >= 0) & (x + dx < NX) & (y + dy >= 0) & (y + dy < NY)
    return plane, depth, swap.reshape(256, 256), inside


def mm(left, right, left_dim=1, right_dim=0):
    return lax.dot_general(
        left, right, (((left_dim,), (right_dim,)), ((), ())), preferred_element_type=F32
    )


def kernel(
    x_in, cot_in, w_in, cw_in, plane_in, depth_in, swap_in, inside_in,
    act_out, grad_out, mode_out, conv_out,
    x, cot, w, cw, plane, depth, swap, inside,
    act, grad, mode, conv,
    send, recv, halo, pre_halo, cols, forward_w, back_w, mix_w, total, pg, layers, cot_layers, act_layers, coef, coef_back,
    part_send, part_recv, term_send, term_recv, full_send, full_recv,
    in_sem, out_sem, send_sem, recv_sem, halo_sem, sum_send_sem, sum_recv_sem,
):
    me_b = lax.axis_index("batch")
    me_s = lax.axis_index("space")
    mine = {"batch": me_b, "space": me_s}
    beside = me_s - me_s % 2

    loads = [
        pltpu.make_async_copy(source, target, in_sem.at[i])
        for i, (source, target) in enumerate(
            (
                (x_in, x), (plane_in, plane), (depth_in, depth), (inside_in, inside),
                (cw_in, cw), (swap_in, swap), (w_in, w), (cot_in, cot),
            )
        )
    ]
    for load in loads:
        load.start()

    barrier = pltpu.get_barrier_semaphore()

    def greet(step, carry):
        for axis in ("space", "batch"):
            peer = lax.rem(mine[axis] + step, G)
            pl.semaphore_signal(barrier, inc=1, device_id={axis: peer}, device_id_type=MESH)
        across = {"batch": lax.rem(me_b + step, G), "space": beside + 1 - me_s % 2}
        pl.semaphore_signal(barrier, inc=1, device_id=across, device_id_type=MESH)
        return carry

    lax.fori_loop(1, G, greet, 0)

    def peer_of(axis, i):
        return lax.rem(mine[axis] + 1 + i, G)

    def tile_copy(phase, axis, source, slot):
        return pltpu.make_async_remote_copy(
            src_ref=send.at[phase, source],
            dst_ref=recv.at[phase, slot],
            send_sem=send_sem.at[phase, source],
            recv_sem=recv_sem.at[phase, slot],
            device_id={axis: source},
            device_id_type=MESH,
        )

    def exchange_start(phase, axis, value):
        me = mine[axis]
        send[phase] = value.reshape(G, 16, 128)
        recv[phase, me] = send[phase, me]

        def step(i, carry):
            tile_copy(phase, axis, peer_of(axis, i), me).start()
            return carry

        lax.fori_loop(0, G - 1, step, 0)

    def exchange_wait(phase, axis):
        me = mine[axis]

        def step(i, carry):
            peer = peer_of(axis, i)
            tile_copy(phase, axis, peer, peer).wait_recv()
            return carry

        lax.fori_loop(0, G - 1, step, 0)
        return recv[phase].reshape(256, 128)

    def exchange_drain(phase, axis):
        me = mine[axis]

        def step(i, carry):
            tile_copy(phase, axis, peer_of(axis, i), me).wait_send()
            return carry

        lax.fori_loop(0, G - 1, step, 0)

    def halo_copy(source, target, slot, which, offset):
        return pltpu.make_async_remote_copy(
            src_ref=source,
            dst_ref=target.at[slot],
            send_sem=halo_sem.at[0, which],
            recv_sem=halo_sem.at[1, which],
            device_id={"space": lax.rem(me_s + offset, G)},
            device_id_type=MESH,
        )

    def depth_transform(which, tiles):
        stacked = jnp.concatenate([tiles[:, :C], tiles[:, C:]], axis=0)
        both = mm(depth[which], stacked)
        return jnp.concatenate([both[:256], both[256:]], axis=1).astype(BF16)

    def spread(layer, cells):
        for tap in range(9):
            shift = (tap // 3 - 1) * NY + (tap % 3 - 1)
            moved = cells
            if shift:
                moved = pltpu.roll(cells, (-shift) % PLANE, 1) * inside[tap : tap + 1, :]
            cols[tap * C : (tap + 1) * C, layer * PLANE : (layer + 1) * PLANE] = moved

    def stencil(weights):
        width = 256
        for chunk in range(PLANE // width):
            lanes = [pl.ds(layer * PLANE + chunk * width, width) for layer in range(4)]
            acc = mm(weights[C : 3 * C, :], cols[:, lanes[1]])
            acc = acc + mm(weights[0 : 2 * C, :], cols[:, lanes[2]])
            first = mm(weights[2 * C : 3 * C, :], cols[:, lanes[0]])
            last = mm(weights[0:C, :], cols[:, lanes[3]])
            total[:, pl.ds(chunk * width, width)] = acc + jnp.concatenate([first, last], axis=0)

    row = lax.broadcasted_iota(jnp.int32, (128, 128), 0)
    column = lax.broadcasted_iota(jnp.int32, (128, 128), 1)
    split = jnp.where(column == lax.rem(row, C) * 2 + row // C, 1.0, 0.0).astype(BF16)

    def by_layer_of(ref):
        return mm(split, ref[...].reshape(128, PLANE)).astype(BF16)

    def by_channel_of(value):
        return mm(split, value, 0, 0).astype(BF16).reshape(C, 2, value.shape[1])

    loads[0].wait()
    loads[1].wait()
    layers[...] = by_layer_of(x)
    plane_coef = mm(plane[...], layers[...], 1, 1).astype(BF16)
    pl.semaphore_wait(barrier, 3 * (G - 1))
    exchange_start(0, "space", plane_coef)
    halos = [
        halo_copy(layers.at[pl.ds(C, C), :], halo, 0, 0, 1),
        halo_copy(layers.at[pl.ds(0, C), :], halo, 1, 1, G - 1),
    ]
    for copy in halos:
        copy.start()

    loads[2].wait()
    loads[3].wait()
    spread(1, layers[:C, :])
    tiles = exchange_wait(0, "space")
    exchange_start(1, "batch", depth_transform(0, tiles))

    loads[4].wait()
    for a in range(3):
        for tap in range(9):
            block = cw[a, tap]
            forward_w[(2 - a) * C : (3 - a) * C, tap * C : (tap + 1) * C] = (
                block.astype(F32).T.astype(BF16)
            )
            back_w[a * C : (a + 1) * C, (8 - tap) * C : (9 - tap) * C] = block
    loads[5].wait()
    loads[6].wait()
    mix_w[...] = jnp.zeros_like(mix_w)
    for p in range(KZ):
        mix_w[p, :C, :C] = w[p]
        mix_w[p, C:, C:] = w[KZ + p]

    tiles = exchange_wait(1, "batch")
    coef[...] = mm(swap[...], tiles).astype(BF16)

    def rows_of(p):
        return pl.ds(p * 16, 16)

    def pad_and_swap(pieces):
        value = jnp.concatenate(pieces + [jnp.zeros((64, 128), F32)], axis=0).astype(BF16)
        return mm(swap[...], value).astype(BF16)

    mixed = [mm(coef[rows_of(p), :], mix_w[p]) for p in range(KZ)]
    exchange_start(2, "batch", pad_and_swap(mixed))

    spread(2, layers[C:, :])
    for copy in halos:
        copy.wait_recv()
    spread(0, jnp.where(me_s > 0, halo[0], jnp.zeros_like(halo[0])))
    spread(3, jnp.where(me_s < G - 1, halo[1], jnp.zeros_like(halo[1])))

    tiles = exchange_wait(2, "batch")
    exchange_start(3, "space", depth_transform(1, tiles))
    stencil(forward_w)
    loads[7].wait()
    cot_layers[...] = by_layer_of(cot)
    tiles = exchange_wait(3, "space")
    doubled = tiles * jnp.asarray(2.0, BF16)

    for chunk in range(4):
        lanes = pl.ds(chunk * 256, 256)
        total[:, lanes] += mm(doubled, plane[:, lanes], 0, 0)
    for layer in range(2):
        for chunk in range(4):
            lanes = pl.ds(chunk * 256, 256)
            rows = pl.ds(layer * C, C)
            pre = total[rows, lanes]
            normal_cdf = 0.5 * (1.0 + lax.erf(pre * inv_root_two))
            density = jnp.exp(-0.5 * pre * pre) * inv_root_two_pi
            act_layers[rows, lanes] = (pre * normal_cdf).astype(BF16)
            pg[rows, lanes] = (
                cot_layers[rows, lanes].astype(F32) * (normal_cdf + pre * density)
            ).astype(BF16)
    back_plane = (mm(plane[...], pg[...], 1, 1) * 2.0).astype(BF16)
    exchange_start(4, "space", back_plane)
    pre_halos = [
        halo_copy(pg.at[pl.ds(C, C), :], pre_halo, 0, 2, 1),
        halo_copy(pg.at[pl.ds(0, C), :], pre_halo, 1, 3, G - 1),
    ]
    for copy in pre_halos:
        copy.start()

    for chunk in range(4):
        lanes = pl.ds(chunk * 256, 256)
        act[:, :, lanes] = by_channel_of(act_layers[:, lanes])
    stores = [pltpu.make_async_copy(act, act_out, out_sem.at[0])]
    stores[0].start()

    for r in range(3):
        rows = pl.ds(r * 192, 192)
        by_layer = [
            mm(cols[rows, pl.ds(layer * PLANE, PLANE)], pg[...], 1, 1) for layer in range(4)
        ]
        terms = [by_layer[a][:, :C] + by_layer[a + 1][:, C:] for a in range(3)]
        part_send[rows, :] = jnp.concatenate(terms[:2], axis=1).astype(BF16)
        part_send[pl.ds(576 + r * 96, 96), :] = jnp.concatenate(
            [terms[2][:96], terms[2][96:]], axis=1
        ).astype(BF16)
    part_send[pl.ds(864, 160), :] = jnp.zeros((160, 128), BF16)

    def part_rows(i):
        return part_send.at[pl.ds(pl.multiple_of(i * 32, 32), 32), :]

    def in_layer(i):
        return {"batch": i // 2, "space": beside + i % 2}

    def in_column(i):
        return {"space": i * 2 + me_s % 2}

    at_layer = me_b * 2 + me_s % 2
    stages = (
        (32, at_layer, in_layer, part_rows, part_recv),
        (8, me_s // 2, in_column, lambda i: term_send, term_recv),
        (32, at_layer, in_layer, lambda i: full_send, full_recv),
    )

    def sum_loop(stage, act_on):
        count, me, device, source, target = stages[stage]

        def step(i, carry):
            peer = lax.rem(me + i, count)
            act_on(peer, me, device, source, target)
            return carry

        lax.fori_loop(1, count, step, 0)

    def sum_copy(stage, peer, slot, device, source, target):
        return pltpu.make_async_remote_copy(
            src_ref=source(peer),
            dst_ref=target.at[slot],
            send_sem=sum_send_sem.at[stage, peer],
            recv_sem=sum_recv_sem.at[stage, slot],
            device_id=device(peer),
            device_id_type=MESH,
        )

    def sum_start(stage):
        count, me, device, source, target = stages[stage]
        target[me] = source(me)[...]
        sum_loop(stage, lambda peer, me, *rest: sum_copy(stage, peer, me, *rest).start())

    def sum_wait(stage):
        sum_loop(stage, lambda peer, me, *rest: sum_copy(stage, peer, peer, *rest).wait_recv())

    def sum_drain(stage):
        sum_loop(stage, lambda peer, me, *rest: sum_copy(stage, peer, me, *rest).wait_send())

    def added(target):
        value = target[0].astype(F32)
        for i in range(1, target.shape[0]):
            value = value + target[i].astype(F32)
        return value

    sum_start(0)
    tiles = exchange_wait(4, "space")
    exchange_start(5, "batch", depth_transform(2, tiles))

    spread(1, pg[:C, :])
    spread(2, pg[C:, :])
    sum_wait(0)
    term_send[...] = added(part_recv).astype(BF16)
    sum_start(1)
    tiles = exchange_wait(5, "batch")
    coef_back[...] = mm(swap[...], tiles).astype(BF16)
    gradients = [mm(coef_back[rows_of(p), :], mix_w[p], 1, 1) for p in range(KZ)]
    exchange_start(6, "batch", pad_and_swap(gradients))

    for p in range(KZ):
        product = mm(coef[rows_of(p), :], coef_back[rows_of(p), :], 0, 0)
        mode[p] = product[:C, :C]
        mode[KZ + p] = product[C:, C:]
    stores.append(pltpu.make_async_copy(mode, mode_out, out_sem.at[1]))
    stores[1].start()

    sum_wait(1)
    full_send[...] = (added(term_recv) * conv_scale).astype(BF16)
    sum_start(2)
    tiles = exchange_wait(6, "batch")
    exchange_start(7, "space", depth_transform(3, tiles))

    for copy in pre_halos:
        copy.wait_recv()
    spread(0, jnp.where(me_s > 0, pre_halo[0], jnp.zeros_like(pre_halo[0])))
    spread(3, jnp.where(me_s < G - 1, pre_halo[1], jnp.zeros_like(pre_halo[1])))
    stencil(back_w)

    tiles = exchange_wait(7, "space")
    for chunk in range(4):
        lanes = pl.ds(chunk * 256, 256)
        value = (total[:, lanes] + mm(tiles, plane[:, lanes], 0, 0)).astype(BF16)
        grad[:, :, lanes] = by_channel_of(value)
    stores.append(pltpu.make_async_copy(grad, grad_out, out_sem.at[2]))
    stores[2].start()

    sum_wait(2)
    for i in range(9):
        value = full_recv[2 * i : 2 * i + 2].reshape(64, 128).astype(F32)
        conv[pl.ds(i * 64, 64), :] = value[:, :C]
        conv[pl.ds(576 + i * 64, 64), :] = value[:, C:]
    for r in range(3):
        value = full_recv[18 + 3 * r : 21 + 3 * r].reshape(96, 128).astype(F32)
        conv[pl.ds(1152 + r * 192, 96), :] = value[:, :C]
        conv[pl.ds(1152 + r * 192 + 96, 96), :] = value[:, C:]
    stores.append(pltpu.make_async_copy(conv, conv_out, out_sem.at[3]))
    stores[3].start()

    for phase, axis in enumerate(("space", "batch", "batch", "space") * 2):
        exchange_drain(phase, axis)
    for stage in range(3):
        sum_drain(stage)
    for copy in halos + pre_halos:
        copy.wait_send()
    for store in stores:
        store.wait()


def deliver(*refs):
    sources, targets, held, (in_sem, out_sem) = refs[:4], refs[4:8], refs[8:12], refs[12:]
    loads = [pltpu.make_async_copy(sources[i], held[i], in_sem.at[i]) for i in range(4)]
    stores = [pltpu.make_async_copy(held[i], targets[i], out_sem.at[i]) for i in range(4)]
    for load in loads:
        load.start()
    for load, store in zip(loads, stores):
        load.wait()
        store.start()
    for store in stores:
        store.wait()


def shards(snapshots, cotangent, mode_weight, conv_weight):
    plane, depth, swap, inside = make_tables()
    any_space = pl.BlockSpec(memory_space=pltpu.HBM)
    vmem = pltpu.VMEM
    dma = pltpu.SemaphoreType.DMA
    outs = pl.pallas_call(
        kernel,
        name="layer",
        out_shape=(
            jax.ShapeDtypeStruct((C, 2, PLANE), BF16),
            jax.ShapeDtypeStruct((C, 2, PLANE), BF16),
            jax.ShapeDtypeStruct((2 * KZ, C, C), F32),
            jax.ShapeDtypeStruct((27 * C, C), F32),
        ),
        in_specs=[any_space] * 8,
        out_specs=(any_space,) * 4,
        scratch_shapes=[
            vmem((C, 2, PLANE), BF16),
            vmem((C, 2, PLANE), BF16),
            vmem((2 * KZ, C, C), BF16),
            vmem((3, 9, C, C), BF16),
            vmem((256, PLANE), BF16),
            vmem((4, 512, 512), BF16),
            vmem((256, 256), BF16),
            vmem((16, PLANE), BF16),
            vmem((C, 2, PLANE), BF16),
            vmem((C, 2, PLANE), BF16),
            vmem((2 * KZ, C, C), F32),
            vmem((27 * C, C), F32),
            vmem((8, G, 16, 128), BF16),
            vmem((8, G, 16, 128), BF16),
            vmem((2, C, PLANE), BF16),
            vmem((2, C, PLANE), BF16),
            vmem((9 * C, 4 * PLANE), BF16),
            vmem((3 * C, 9 * C), BF16),
            vmem((3 * C, 9 * C), BF16),
            vmem((KZ, 128, 128), BF16),
            vmem((128, PLANE), F32),
            vmem((128, PLANE), BF16),
            vmem((128, PLANE), BF16),
            vmem((128, PLANE), BF16),
            vmem((128, PLANE), BF16),
            vmem((256, 128), BF16),
            vmem((256, 128), BF16),
            vmem((1024, 128), BF16),
            vmem((32, 32, 128), BF16),
            vmem((32, 128), BF16),
            vmem((8, 32, 128), BF16),
            vmem((32, 128), BF16),
            vmem((32, 32, 128), BF16),
            dma((8,)),
            dma((4,)),
            dma((8, G)),
            dma((8, G)),
            dma((2, 4)),
            dma((3, 32)),
            dma((3, 32)),
        ],
        compiler_params=pltpu.CompilerParams(
            collective_id=0, has_side_effects=True, vmem_limit_bytes=60 << 20
        ),
    )(
        snapshots[0],
        cotangent[0],
        mode_weight.reshape(2 * KZ, C, C),
        conv_weight.reshape(3, 9, C, C),
        jnp.asarray(plane),
        jnp.asarray(depth),
        jnp.asarray(swap),
        jnp.asarray(inside),
    )
    outs = pl.pallas_call(
        deliver,
        name="deliver",
        out_shape=tuple(jax.ShapeDtypeStruct(out.shape, out.dtype) for out in outs),
        in_specs=[any_space] * 4,
        out_specs=(any_space,) * 4,
        scratch_shapes=[vmem(out.shape, out.dtype) for out in outs] + [dma((4,)), dma((4,))],
        compiler_params=pltpu.CompilerParams(vmem_limit_bytes=60 << 20),
    )(*outs)
    activated, input_gradient, mode_gradient, conv_gradient = outs
    return (
        activated.reshape(1, C, 2, PLANE),
        input_gradient.reshape(1, C, 2, PLANE),
        mode_gradient.reshape(1, 1, 2 * KZ, C, C),
        conv_gradient.reshape(3, 3, 3, C, C),
    )


def solution(mesh):
    in_specs = (
        P("batch", None, "space", None),
        P("batch", None, "space", None),
        P("batch", "space", None, None, None),
        P(),
    )
    out_specs = in_specs
    return jax.shard_map(shards, mesh=mesh, in_specs=in_specs, out_specs=out_specs, check_vma=False)
```

```python
import math

import jax
import jax.numpy as jnp
import ml_dtypes
import numpy as np
from jax import lax
from jax.experimental import pallas as pl
from jax.experimental.pallas import tpu as pltpu
from jax.sharding import PartitionSpec as P

KX = 8
KY = 8
KZ = 12
NX = 32
NY = 32
NZ = 32
PLANE = NX * NY
C = 64
G = 16
SNAPS = 16

MESH = pl.DeviceIdType.MESH
F32 = jnp.float32
BF16 = jnp.bfloat16

inv_root_two = 1.0 / math.sqrt(2.0)
inv_root_two_pi = 1.0 / math.sqrt(2.0 * math.pi)
conv_scale = 1.0 / math.sqrt(SNAPS * NZ * PLANE)


def basis_rows(half_count, length):
    rows = np.arange(2 * half_count)[:, None]
    cells = np.arange(length)[None, :]
    frequency = np.where(rows < half_count, rows, rows - half_count + 1)
    phases = ((frequency * cells) % length).astype(np.float32) * np.float32(2.0 * math.pi / length)
    return np.where(rows < half_count, np.cos(phases), np.sin(phases)).astype(np.float32)


def make_tables():
    across = basis_rows(KX, NX)
    along_y = basis_rows(KY, NY)
    depth_rows = basis_rows(KZ, NZ)
    outer = across[None, :, :, None] * along_y[:, None, None, :]
    plane = (outer.reshape(256, PLANE) * np.float32(2.0 / math.sqrt(PLANE))).astype(ml_dtypes.bfloat16)
    analysis = (depth_rows * np.float32(math.sqrt(2.0 / NZ))).astype(ml_dtypes.bfloat16)
    synthesis = (depth_rows.T * np.float32(math.sqrt(2.0 / (2 * KZ)))).astype(ml_dtypes.bfloat16)
    to_modes = np.zeros((2, G, 16, 2, G, 16), ml_dtypes.bfloat16)
    to_cells = np.zeros((2, G, 16, 2, G, 16), ml_dtypes.bfloat16)
    down = analysis.reshape(2, KZ, 16, 2).transpose(0, 1, 3, 2)
    up = synthesis.reshape(16, 2, 2, KZ).transpose(1, 0, 2, 3)
    for mode in range(16):
        to_modes[:, mode, :KZ, :, :, mode] = down
        to_cells[:, :, mode, :, mode, :KZ] = up
    to_modes = to_modes.reshape(512, 512)
    to_cells = to_cells.reshape(512, 512)
    depth = np.stack([to_modes, to_cells, to_cells.T, to_modes.T])
    swap = np.zeros((16, 16, 16, 16), ml_dtypes.bfloat16)
    for a in range(16):
        for b in range(16):
            swap[a, b, b, a] = 1
    x = np.arange(PLANE) // NY
    y = np.arange(PLANE) % NY
    inside = np.zeros((16, PLANE), ml_dtypes.bfloat16)
    for tap in range(9):
        dx, dy = tap // 3 - 1, tap % 3 - 1
        inside[tap] = (x + dx >= 0) & (x + dx < NX) & (y + dy >= 0) & (y + dy < NY)
    return plane, depth, swap.reshape(256, 256), inside


def mm(left, right, left_dim=1, right_dim=0):
    return lax.dot_general(
        left, right, (((left_dim,), (right_dim,)), ((), ())), preferred_element_type=F32
    )


def kernel(
    x_in, cot_in, w_in, cw_in, plane_in, depth_in, swap_in, inside_in,
    act_out, grad_out, mode_out, conv_out,
    x, cot, w, cw, plane, depth, swap, inside,
    act, grad, mode, conv,
    send, recv, halo, pre_halo, cols, forward_w, back_w, mix_w, unmix_w, total, pg, layers, cot_layers, act_layers, coef, coef_back,
    part_send, part_recv, term_send, term_recv, full_send, full_recv,
    in_sem, out_sem, send_sem, recv_sem, halo_sem, sum_send_sem, sum_recv_sem,
):
    me_b = lax.axis_index("batch")
    me_s = lax.axis_index("space")
    mine = {"batch": me_b, "space": me_s}
    beside = me_s - me_s % 2

    loads = [
        pltpu.make_async_copy(source, target, in_sem.at[i])
        for i, (source, target) in enumerate(
            (
                (x_in, x), (plane_in, plane), (depth_in, depth), (inside_in, inside),
                (cw_in, cw), (swap_in, swap), (w_in, w), (cot_in, cot),
            )
        )
    ]
    for load in loads:
        load.start()

    barrier = pltpu.get_barrier_semaphore()

    def greet(step, carry):
        for axis in ("space", "batch"):
            peer = lax.rem(mine[axis] + step, G)
            pl.semaphore_signal(barrier, inc=1, device_id={axis: peer}, device_id_type=MESH)
        across = {"batch": lax.rem(me_b + step, G), "space": beside + 1 - me_s % 2}
        pl.semaphore_signal(barrier, inc=1, device_id=across, device_id_type=MESH)
        return carry

    lax.fori_loop(1, G, greet, 0)

    def peer_of(axis, i):
        return lax.rem(mine[axis] + 1 + i, G)

    def tile_copy(phase, axis, source, slot):
        return pltpu.make_async_remote_copy(
            src_ref=send.at[phase, source],
            dst_ref=recv.at[phase, slot],
            send_sem=send_sem.at[phase],
            recv_sem=recv_sem.at[phase],
            device_id={axis: source},
            device_id_type=MESH,
        )

    def exchange_start(phase, axis, value):
        me = mine[axis]
        send[phase] = value.reshape(G, 16, 128)
        recv[phase, me] = send[phase, me]

        def step(i, carry):
            tile_copy(phase, axis, peer_of(axis, i), me).start()
            return carry

        lax.fori_loop(0, G - 1, step, 0)

    def all_bytes(buffer, sem):
        others = buffer.at[pl.ds(0, buffer.shape[0] - 1)]
        pltpu.make_async_copy(others, others, sem).wait()

    def exchange_wait(phase):
        all_bytes(recv.at[phase], recv_sem.at[phase])
        return recv[phase].reshape(256, 128)

    def exchange_drain(phase):
        all_bytes(send.at[phase], send_sem.at[phase])

    def halo_copy(source, target, slot, which, offset):
        return pltpu.make_async_remote_copy(
            src_ref=source,
            dst_ref=target.at[slot],
            send_sem=halo_sem.at[0, which],
            recv_sem=halo_sem.at[1, which],
            device_id={"space": lax.rem(me_s + offset, G)},
            device_id_type=MESH,
        )

    def depth_transform(which, tiles):
        stacked = jnp.concatenate([tiles[:, :C], tiles[:, C:]], axis=0)
        both = mm(depth[which], stacked)
        return jnp.concatenate([both[:256], both[256:]], axis=1).astype(BF16)

    def spread(layer, cells):
        for tap in range(9):
            shift = (tap // 3 - 1) * NY + (tap % 3 - 1)
            moved = cells
            if shift:
                moved = pltpu.roll(cells, (-shift) % PLANE, 1) * inside[tap : tap + 1, :]
            cols[tap * C : (tap + 1) * C, layer * PLANE : (layer + 1) * PLANE] = moved

    def stencil(weights):
        width = 256
        for chunk in range(PLANE // width):
            lanes = [pl.ds(layer * PLANE + chunk * width, width) for layer in range(4)]
            acc = mm(weights[C : 3 * C, :], cols[:, lanes[1]])
            acc = acc + mm(weights[0 : 2 * C, :], cols[:, lanes[2]])
            first = mm(weights[2 * C : 3 * C, :], cols[:, lanes[0]])
            last = mm(weights[0:C, :], cols[:, lanes[3]])
            total[:, pl.ds(chunk * width, width)] = acc + jnp.concatenate([first, last], axis=0)

    row = lax.broadcasted_iota(jnp.int32, (128, 128), 0)
    column = lax.broadcasted_iota(jnp.int32, (128, 128), 1)
    split = jnp.where(column == lax.rem(row, C) * 2 + row // C, 1.0, 0.0).astype(BF16)

    def by_layer_of(ref):
        return mm(split, ref[...].reshape(128, PLANE)).astype(BF16)

    def by_channel_of(value):
        return mm(split, value, 0, 0).astype(BF16).reshape(C, 2, value.shape[1])

    loads[0].wait()
    loads[1].wait()
    layers[...] = by_layer_of(x)
    plane_coef = mm(plane[...], layers[...], 1, 1).astype(BF16)
    pl.semaphore_wait(barrier, 3 * (G - 1))
    exchange_start(0, "space", plane_coef)
    halos = [
        halo_copy(layers.at[pl.ds(C, C), :], halo, 0, 0, 1),
        halo_copy(layers.at[pl.ds(0, C), :], halo, 1, 1, G - 1),
    ]
    for copy in halos:
        copy.start()

    loads[2].wait()
    loads[3].wait()
    spread(1, layers[:C, :])
    tiles = exchange_wait(0)
    exchange_start(1, "batch", depth_transform(0, tiles))

    loads[4].wait()
    for a in range(3):
        for tap in range(9):
            block = cw[a, tap]
            forward_w[(2 - a) * C : (3 - a) * C, tap * C : (tap + 1) * C] = (
                block.astype(F32).T.astype(BF16)
            )
            back_w[a * C : (a + 1) * C, (8 - tap) * C : (9 - tap) * C] = block
    loads[5].wait()
    loads[6].wait()
    mix_w[...] = jnp.zeros_like(mix_w)
    for p in range(KZ):
        mix_w[p, :C, :C] = w[p]
        mix_w[p, C:, C:] = w[KZ + p]

    z_mode = lax.broadcasted_iota(jnp.int32, (256, 128), 0) % 16

    def mix(tiles, weights):
        picked = [
            tiles * jnp.where(z_mode == p, 1.0, 0.0).astype(BF16) for p in range(KZ)
        ]
        return mm(jnp.concatenate(picked, axis=1), weights[...].reshape(KZ * 128, 128)).astype(BF16)

    tiles = exchange_wait(1)
    exchange_start(2, "batch", mix(tiles, mix_w))
    coef[...] = mm(swap[...], tiles).astype(BF16)
    for p in range(KZ):
        unmix_w[p] = mix_w[p].astype(F32).T.astype(BF16)

    spread(2, layers[C:, :])
    for copy in halos:
        copy.wait_recv()
    spread(0, jnp.where(me_s > 0, halo[0], jnp.zeros_like(halo[0])))
    spread(3, jnp.where(me_s < G - 1, halo[1], jnp.zeros_like(halo[1])))

    tiles = exchange_wait(2)
    exchange_start(3, "space", depth_transform(1, tiles))
    stencil(forward_w)
    loads[7].wait()
    cot_layers[...] = by_layer_of(cot)
    tiles = exchange_wait(3)
    doubled = tiles * jnp.asarray(2.0, BF16)

    for chunk in range(4):
        lanes = pl.ds(chunk * 256, 256)
        total[:, lanes] += mm(doubled, plane[:, lanes], 0, 0)
    for layer in range(2):
        for chunk in range(4):
            lanes = pl.ds(chunk * 256, 256)
            rows = pl.ds(layer * C, C)
            pre = total[rows, lanes]
            normal_cdf = 0.5 * (1.0 + lax.erf(pre * inv_root_two))
            density = jnp.exp(-0.5 * pre * pre) * inv_root_two_pi
            act_layers[rows, lanes] = (pre * normal_cdf).astype(BF16)
            pg[rows, lanes] = (
                cot_layers[rows, lanes].astype(F32) * (normal_cdf + pre * density)
            ).astype(BF16)
    back_plane = (mm(plane[...], pg[...], 1, 1) * 2.0).astype(BF16)
    exchange_start(4, "space", back_plane)
    pre_halos = [
        halo_copy(pg.at[pl.ds(C, C), :], pre_halo, 0, 2, 1),
        halo_copy(pg.at[pl.ds(0, C), :], pre_halo, 1, 3, G - 1),
    ]
    for copy in pre_halos:
        copy.start()

    for chunk in range(4):
        lanes = pl.ds(chunk * 256, 256)
        act[:, :, lanes] = by_channel_of(act_layers[:, lanes])
    stores = [pltpu.make_async_copy(act, act_out, out_sem.at[0])]
    stores[0].start()

    for r in range(3):
        rows = pl.ds(r * 192, 192)
        by_layer = [
            mm(cols[rows, pl.ds(layer * PLANE, PLANE)], pg[...], 1, 1) for layer in range(4)
        ]
        terms = [by_layer[a][:, :C] + by_layer[a + 1][:, C:] for a in range(3)]
        part_send[rows, :] = jnp.concatenate(terms[:2], axis=1).astype(BF16)
        part_send[pl.ds(576 + r * 96, 96), :] = jnp.concatenate(
            [terms[2][:96], terms[2][96:]], axis=1
        ).astype(BF16)
    part_send[pl.ds(864, 160), :] = jnp.zeros((160, 128), BF16)

    def part_rows(i):
        return part_send.at[pl.ds(pl.multiple_of(i * 32, 32), 32), :]

    def in_layer(i):
        return {"batch": i // 2, "space": beside + i % 2}

    def in_column(i):
        return {"space": i * 2 + me_s % 2}

    at_layer = me_b * 2 + me_s % 2
    stages = (
        (32, at_layer, in_layer, part_rows, part_recv),
        (8, me_s // 2, in_column, lambda i: term_send, term_recv),
        (32, at_layer, in_layer, lambda i: full_send, full_recv),
    )

    def sum_start(stage):
        count, me, device, source, target = stages[stage]
        target[me] = source(me)[...]

        def step(i, carry):
            peer = lax.rem(me + i, count)
            pltpu.make_async_remote_copy(
                src_ref=source(peer),
                dst_ref=target.at[me],
                send_sem=sum_send_sem.at[stage],
                recv_sem=sum_recv_sem.at[stage],
                device_id=device(peer),
                device_id_type=MESH,
            ).start()
            return carry

        lax.fori_loop(1, count, step, 0)

    def sum_wait(stage):
        all_bytes(stages[stage][4], sum_recv_sem.at[stage])

    def sum_drain(stage):
        all_bytes(stages[stage][4], sum_send_sem.at[stage])

    def added(target):
        value = target[0].astype(F32)
        for i in range(1, target.shape[0]):
            value = value + target[i].astype(F32)
        return value

    sum_start(0)
    tiles = exchange_wait(4)
    exchange_start(5, "batch", depth_transform(2, tiles))

    spread(1, pg[:C, :])
    spread(2, pg[C:, :])
    sum_wait(0)
    term_send[...] = added(part_recv).astype(BF16)
    sum_start(1)
    tiles = exchange_wait(5)
    exchange_start(6, "batch", mix(tiles, unmix_w))

    coef_back[...] = mm(swap[...], tiles).astype(BF16)

    def rows_of(p):
        return pl.ds(p * 16, 16)

    for p in range(KZ):
        product = mm(coef[rows_of(p), :], coef_back[rows_of(p), :], 0, 0)
        mode[p] = product[:C, :C]
        mode[KZ + p] = product[C:, C:]
    stores.append(pltpu.make_async_copy(mode, mode_out, out_sem.at[1]))
    stores[1].start()

    sum_wait(1)
    full_send[...] = (added(term_recv) * conv_scale).astype(BF16)
    sum_start(2)
    tiles = exchange_wait(6)
    exchange_start(7, "space", depth_transform(3, tiles))

    for copy in pre_halos:
        copy.wait_recv()
    spread(0, jnp.where(me_s > 0, pre_halo[0], jnp.zeros_like(pre_halo[0])))
    spread(3, jnp.where(me_s < G - 1, pre_halo[1], jnp.zeros_like(pre_halo[1])))
    stencil(back_w)

    tiles = exchange_wait(7)
    for chunk in range(4):
        lanes = pl.ds(chunk * 256, 256)
        value = (total[:, lanes] + mm(tiles, plane[:, lanes], 0, 0)).astype(BF16)
        grad[:, :, lanes] = by_channel_of(value)
    stores.append(pltpu.make_async_copy(grad, grad_out, out_sem.at[2]))
    stores[2].start()

    sum_wait(2)
    for i in range(9):
        value = full_recv[2 * i : 2 * i + 2].reshape(64, 128).astype(F32)
        conv[pl.ds(i * 64, 64), :] = value[:, :C]
        conv[pl.ds(576 + i * 64, 64), :] = value[:, C:]
    for r in range(3):
        value = full_recv[18 + 3 * r : 21 + 3 * r].reshape(96, 128).astype(F32)
        conv[pl.ds(1152 + r * 192, 96), :] = value[:, :C]
        conv[pl.ds(1152 + r * 192 + 96, 96), :] = value[:, C:]
    stores.append(pltpu.make_async_copy(conv, conv_out, out_sem.at[3]))
    stores[3].start()

    for phase in range(8):
        exchange_drain(phase)
    for stage in range(3):
        sum_drain(stage)
    for copy in halos + pre_halos:
        copy.wait_send()
    for store in stores:
        store.wait()


def deliver(*refs):
    sources, targets, held, (in_sem, out_sem) = refs[:4], refs[4:8], refs[8:12], refs[12:]
    loads = [pltpu.make_async_copy(sources[i], held[i], in_sem.at[i]) for i in range(4)]
    stores = [pltpu.make_async_copy(held[i], targets[i], out_sem.at[i]) for i in range(4)]
    for load in loads:
        load.start()
    for load, store in zip(loads, stores):
        load.wait()
        store.start()
    for store in stores:
        store.wait()


def shards(snapshots, cotangent, mode_weight, conv_weight):
    plane, depth, swap, inside = make_tables()
    any_space = pl.BlockSpec(memory_space=pltpu.HBM)
    vmem = pltpu.VMEM
    dma = pltpu.SemaphoreType.DMA
    outs = pl.pallas_call(
        kernel,
        name="layer",
        out_shape=(
            jax.ShapeDtypeStruct((C, 2, PLANE), BF16),
            jax.ShapeDtypeStruct((C, 2, PLANE), BF16),
            jax.ShapeDtypeStruct((2 * KZ, C, C), F32),
            jax.ShapeDtypeStruct((27 * C, C), F32),
        ),
        in_specs=[any_space] * 8,
        out_specs=(any_space,) * 4,
        scratch_shapes=[
            vmem((C, 2, PLANE), BF16),
            vmem((C, 2, PLANE), BF16),
            vmem((2 * KZ, C, C), BF16),
            vmem((3, 9, C, C), BF16),
            vmem((256, PLANE), BF16),
            vmem((4, 512, 512), BF16),
            vmem((256, 256), BF16),
            vmem((16, PLANE), BF16),
            vmem((C, 2, PLANE), BF16),
            vmem((C, 2, PLANE), BF16),
            vmem((2 * KZ, C, C), F32),
            vmem((27 * C, C), F32),
            vmem((8, G, 16, 128), BF16),
            vmem((8, G, 16, 128), BF16),
            vmem((2, C, PLANE), BF16),
            vmem((2, C, PLANE), BF16),
            vmem((9 * C, 4 * PLANE), BF16),
            vmem((3 * C, 9 * C), BF16),
            vmem((3 * C, 9 * C), BF16),
            vmem((KZ, 128, 128), BF16),
            vmem((KZ, 128, 128), BF16),
            vmem((128, PLANE), F32),
            vmem((128, PLANE), BF16),
            vmem((128, PLANE), BF16),
            vmem((128, PLANE), BF16),
            vmem((128, PLANE), BF16),
            vmem((256, 128), BF16),
            vmem((256, 128), BF16),
            vmem((1024, 128), BF16),
            vmem((32, 32, 128), BF16),
            vmem((32, 128), BF16),
            vmem((8, 32, 128), BF16),
            vmem((32, 128), BF16),
            vmem((32, 32, 128), BF16),
            dma((8,)),
            dma((4,)),
            dma((8,)),
            dma((8,)),
            dma((2, 4)),
            dma((3,)),
            dma((3,)),
        ],
        compiler_params=pltpu.CompilerParams(
            collective_id=0, has_side_effects=True, vmem_limit_bytes=60 << 20
        ),
    )(
        snapshots[0],
        cotangent[0],
        mode_weight.reshape(2 * KZ, C, C),
        conv_weight.reshape(3, 9, C, C),
        jnp.asarray(plane),
        jnp.asarray(depth),
        jnp.asarray(swap),
        jnp.asarray(inside),
    )
    outs = pl.pallas_call(
        deliver,
        name="deliver",
        out_shape=tuple(jax.ShapeDtypeStruct(out.shape, out.dtype) for out in outs),
        in_specs=[any_space] * 4,
        out_specs=(any_space,) * 4,
        scratch_shapes=[vmem(out.shape, out.dtype) for out in outs] + [dma((4,)), dma((4,))],
        compiler_params=pltpu.CompilerParams(vmem_limit_bytes=60 << 20),
    )(*outs)
    activated, input_gradient, mode_gradient, conv_gradient = outs
    return (
        activated.reshape(1, C, 2, PLANE),
        input_gradient.reshape(1, C, 2, PLANE),
        mode_gradient.reshape(1, 1, 2 * KZ, C, C),
        conv_gradient.reshape(3, 3, 3, C, C),
    )


def solution(mesh):
    in_specs = (
        P("batch", None, "space", None),
        P("batch", None, "space", None),
        P("batch", "space", None, None, None),
        P(),
    )
    out_specs = in_specs
    return jax.shard_map(shards, mesh=mesh, in_specs=in_specs, out_specs=out_specs, check_vma=False)
```

```python
import math

import jax
import jax.numpy as jnp
import ml_dtypes
import numpy as np
from jax import lax
from jax.experimental import pallas as pl
from jax.experimental.pallas import tpu as pltpu
from jax.sharding import PartitionSpec as P

KX = 8
KY = 8
KZ = 12
NX = 32
NY = 32
NZ = 32
PLANE = NX * NY
C = 64
G = 16
SNAPS = 16

MESH = pl.DeviceIdType.MESH
F32 = jnp.float32
BF16 = jnp.bfloat16

inv_root_two = 1.0 / math.sqrt(2.0)
inv_root_two_pi = 1.0 / math.sqrt(2.0 * math.pi)
conv_scale = 1.0 / math.sqrt(SNAPS * NZ * PLANE)


def basis_rows(half_count, length):
    rows = np.arange(2 * half_count)[:, None]
    cells = np.arange(length)[None, :]
    frequency = np.where(rows < half_count, rows, rows - half_count + 1)
    phases = ((frequency * cells) % length).astype(np.float32) * np.float32(2.0 * math.pi / length)
    return np.where(rows < half_count, np.cos(phases), np.sin(phases)).astype(np.float32)


def make_tables():
    across = basis_rows(KX, NX)
    along_y = basis_rows(KY, NY)
    depth_rows = basis_rows(KZ, NZ)
    outer = across[None, :, :, None] * along_y[:, None, None, :]
    plane = (outer.reshape(256, PLANE) * np.float32(2.0 / math.sqrt(PLANE))).astype(ml_dtypes.bfloat16)
    analysis = (depth_rows * np.float32(math.sqrt(2.0 / NZ))).astype(ml_dtypes.bfloat16)
    synthesis = (depth_rows.T * np.float32(math.sqrt(2.0 / (2 * KZ)))).astype(ml_dtypes.bfloat16)
    to_modes = np.zeros((2, G, 16, 2, G, 16), ml_dtypes.bfloat16)
    to_cells = np.zeros((2, G, 16, 2, G, 16), ml_dtypes.bfloat16)
    down = analysis.reshape(2, KZ, 16, 2).transpose(0, 1, 3, 2)
    up = synthesis.reshape(16, 2, 2, KZ).transpose(1, 0, 2, 3)
    for mode in range(16):
        to_modes[:, mode, :KZ, :, :, mode] = down
        to_cells[:, :, mode, :, mode, :KZ] = up
    to_modes = to_modes.reshape(512, 512)
    to_cells = to_cells.reshape(512, 512)
    depth = np.stack([to_modes, to_cells, to_cells.T, to_modes.T])
    swap = np.zeros((16, 16, 16, 16), ml_dtypes.bfloat16)
    for a in range(16):
        for b in range(16):
            swap[a, b, b, a] = 1
    x = np.arange(PLANE) // NY
    y = np.arange(PLANE) % NY
    inside = np.zeros((16, PLANE), ml_dtypes.bfloat16)
    for tap in range(9):
        dx, dy = tap // 3 - 1, tap % 3 - 1
        inside[tap] = (x + dx >= 0) & (x + dx < NX) & (y + dy >= 0) & (y + dy < NY)
    return plane, depth, swap.reshape(256, 256), inside


def mm(left, right, left_dim=1, right_dim=0):
    return lax.dot_general(
        left, right, (((left_dim,), (right_dim,)), ((), ())), preferred_element_type=F32
    )


def kernel(
    x_in, cot_in, w_in, cw_in, plane_in, depth_in, swap_in, inside_in,
    act_out, grad_out, mode_out, conv_out,
    x, cot, w, cw, plane, depth, swap, inside,
    act, grad, mode,
    send, recv, halo, pre_halo, cols, forward_w, back_w, mix_w, unmix_w, total, pg, layers, cot_layers, act_layers, coef, coef_back,
    part_send, part_recv, term_send, term_recv, full_send, full_recv,
    in_sem, out_sem, send_sem, recv_sem, halo_sem, sum_send_sem, sum_recv_sem,
):
    me_b = lax.axis_index("batch")
    me_s = lax.axis_index("space")
    mine = {"batch": me_b, "space": me_s}
    beside = me_s - me_s % 2

    barrier = pltpu.get_barrier_semaphore()
    for step in (8, 7, 9, 6, 10, 5, 11, 4, 12, 3, 13, 2, 14, 1, 15):
        peer_b, peer_s = lax.rem(me_b + step, G), lax.rem(me_s + step, G)
        for target in (
            {"space": peer_s}, {"batch": peer_b}, {"batch": peer_b, "space": beside + 1 - me_s % 2},
        ):
            pl.semaphore_signal(barrier, inc=1, device_id=target, device_id_type=MESH)

    loads = [
        pltpu.make_async_copy(source, target, in_sem.at[i])
        for i, (source, target) in enumerate(
            (
                (x_in, x), (plane_in, plane), (depth_in, depth), (inside_in, inside),
                (cw_in, cw), (swap_in, swap), (w_in, w), (cot_in, cot),
            )
        )
    ]
    for load in loads:
        load.start()

    def peer_of(axis, i):
        return lax.rem(mine[axis] + 1 + i, G)

    def tile_copy(phase, axis, source, slot):
        return pltpu.make_async_remote_copy(
            src_ref=send.at[phase, source],
            dst_ref=recv.at[phase, slot],
            send_sem=send_sem.at[phase],
            recv_sem=recv_sem.at[phase],
            device_id={axis: source},
            device_id_type=MESH,
        )

    def exchange_start(phase, axis, value):
        me = mine[axis]
        send[phase] = value.reshape(G, 16, 128)

        def step(i, carry):
            tile_copy(phase, axis, peer_of(axis, i), me).start()
            return carry

        lax.fori_loop(0, G - 1, step, 0)
        recv[phase, me] = send[phase, me]

    def all_bytes(buffer, sem):
        others = buffer.at[pl.ds(0, buffer.shape[0] - 1)]
        pltpu.make_async_copy(others, others, sem).wait()

    def exchange_wait(phase):
        all_bytes(recv.at[phase], recv_sem.at[phase])
        return recv[phase].reshape(256, 128)

    def exchange_drain(phase):
        all_bytes(send.at[phase], send_sem.at[phase])

    def halo_copy(source, target, slot, which, offset):
        return pltpu.make_async_remote_copy(
            src_ref=source,
            dst_ref=target.at[slot],
            send_sem=halo_sem.at[0, which],
            recv_sem=halo_sem.at[1, which],
            device_id={"space": lax.rem(me_s + offset, G)},
            device_id_type=MESH,
        )

    def depth_transform(which, tiles):
        stacked = jnp.concatenate([tiles[:, :C], tiles[:, C:]], axis=0)
        both = mm(depth[which], stacked)
        return jnp.concatenate([both[:256], both[256:]], axis=1).astype(BF16)

    def spread(layer, cells):
        for tap in range(9):
            shift = (tap // 3 - 1) * NY + (tap % 3 - 1)
            moved = cells
            if shift:
                moved = pltpu.roll(cells, (-shift) % PLANE, 1) * inside[tap : tap + 1, :]
            cols[tap * C : (tap + 1) * C, layer * PLANE : (layer + 1) * PLANE] = moved

    def stencil(weights):
        width = 256
        for chunk in range(PLANE // width):
            lanes = [pl.ds(layer * PLANE + chunk * width, width) for layer in range(4)]
            acc = mm(weights[C : 3 * C, :], cols[:, lanes[1]])
            acc = acc + mm(weights[0 : 2 * C, :], cols[:, lanes[2]])
            first = mm(weights[2 * C : 3 * C, :], cols[:, lanes[0]])
            last = mm(weights[0:C, :], cols[:, lanes[3]])
            total[:, pl.ds(chunk * width, width)] = acc + jnp.concatenate([first, last], axis=0)

    row = lax.broadcasted_iota(jnp.int32, (128, 128), 0)
    column = lax.broadcasted_iota(jnp.int32, (128, 128), 1)
    split = jnp.where(column == lax.rem(row, C) * 2 + row // C, 1.0, 0.0).astype(BF16)

    def by_layer_of(ref):
        return mm(split, ref[...].reshape(128, PLANE)).astype(BF16)

    def by_channel_of(value):
        return mm(split, value, 0, 0).astype(BF16).reshape(C, 2, value.shape[1])

    loads[0].wait()
    loads[1].wait()
    layers[...] = by_layer_of(x)
    plane_coef = mm(plane[...], layers[...], 1, 1).astype(BF16)
    pl.semaphore_wait(barrier, 3 * (G - 1))
    exchange_start(0, "space", plane_coef)
    halos = [
        halo_copy(layers.at[pl.ds(C, C), :], halo, 0, 0, 1),
        halo_copy(layers.at[pl.ds(0, C), :], halo, 1, 1, G - 1),
    ]
    halos[0].start()

    loads[2].wait()
    loads[3].wait()
    spread(1, layers[:C, :])
    tiles = exchange_wait(0)
    exchange_start(1, "batch", depth_transform(0, tiles))
    halos[1].start()

    loads[4].wait()
    for a in range(3):
        for tap in range(9):
            block = cw[a, tap]
            forward_w[(2 - a) * C : (3 - a) * C, tap * C : (tap + 1) * C] = (
                block.astype(F32).T.astype(BF16)
            )
            back_w[a * C : (a + 1) * C, (8 - tap) * C : (9 - tap) * C] = block
    loads[5].wait()
    loads[6].wait()
    mix_w[...] = jnp.zeros_like(mix_w)
    for p in range(KZ):
        mix_w[p, :C, :C] = w[p]
        mix_w[p, C:, C:] = w[KZ + p]

    z_mode = lax.broadcasted_iota(jnp.int32, (256, 128), 0) % 16

    def mix(tiles, weights):
        picked = [
            tiles * jnp.where(z_mode == p, 1.0, 0.0).astype(BF16) for p in range(KZ)
        ]
        return mm(jnp.concatenate(picked, axis=1), weights[...].reshape(KZ * 128, 128)).astype(BF16)

    tiles = exchange_wait(1)
    exchange_start(2, "batch", mix(tiles, mix_w))
    coef[...] = mm(swap[...], tiles).astype(BF16)
    for p in range(KZ):
        unmix_w[p] = mix_w[p].astype(F32).T.astype(BF16)

    spread(2, layers[C:, :])
    for copy in halos:
        copy.wait_recv()
    spread(0, jnp.where(me_s > 0, halo[0], jnp.zeros_like(halo[0])))
    spread(3, jnp.where(me_s < G - 1, halo[1], jnp.zeros_like(halo[1])))

    tiles = exchange_wait(2)
    exchange_start(3, "space", depth_transform(1, tiles))
    stencil(forward_w)
    loads[7].wait()
    cot_layers[...] = by_layer_of(cot)
    tiles = exchange_wait(3)
    doubled = tiles * jnp.asarray(2.0, BF16)

    for chunk in range(4):
        lanes = pl.ds(chunk * 256, 256)
        total[:, lanes] += mm(doubled, plane[:, lanes], 0, 0)
    for layer in range(2):
        for chunk in range(4):
            lanes = pl.ds(chunk * 256, 256)
            rows = pl.ds(layer * C, C)
            pre = total[rows, lanes]
            normal_cdf = 0.5 * (1.0 + lax.erf(pre * inv_root_two))
            density = jnp.exp(-0.5 * pre * pre) * inv_root_two_pi
            act_layers[rows, lanes] = (pre * normal_cdf).astype(BF16)
            pg[rows, lanes] = (
                cot_layers[rows, lanes].astype(F32) * (normal_cdf + pre * density)
            ).astype(BF16)
    back_plane = (mm(plane[...], pg[...], 1, 1) * 2.0).astype(BF16)
    exchange_start(4, "space", back_plane)
    pre_halos = [
        halo_copy(pg.at[pl.ds(C, C), :], pre_halo, 0, 2, 1),
        halo_copy(pg.at[pl.ds(0, C), :], pre_halo, 1, 3, G - 1),
    ]
    pre_halos[0].start()

    for r in range(3):
        rows = pl.ds(r * 192, 192)
        by_layer = [
            mm(cols[rows, pl.ds(layer * PLANE, PLANE)], pg[...], 1, 1) for layer in range(4)
        ]
        terms = [by_layer[a][:, :C] + by_layer[a + 1][:, C:] for a in range(3)]
        part_send[rows, :] = jnp.concatenate(terms[:2], axis=1).astype(BF16)
        part_send[pl.ds(576 + r * 96, 96), :] = jnp.concatenate(
            [terms[2][:96], terms[2][96:]], axis=1
        ).astype(BF16)
    part_send[pl.ds(864, 160), :] = jnp.zeros((160, 128), BF16)

    def part_rows(i):
        return part_send.at[pl.ds(pl.multiple_of(i * 32, 32), 32), :]

    def in_layer(i):
        return {"batch": i // 2, "space": beside + i % 2}

    def in_column(i):
        return {"space": i * 2 + me_s % 2}

    at_layer = me_b * 2 + me_s % 2
    stages = (
        (32, at_layer, in_layer, part_rows, part_recv),
        (8, me_s // 2, in_column, lambda i: term_send, term_recv),
        (32, at_layer, in_layer, lambda i: full_send, full_recv),
    )

    def sum_start(stage):
        count, me, device, source, target = stages[stage]
        target[me] = source(me)[...]

        def step(i, carry):
            peer = lax.rem(me + i, count)
            pltpu.make_async_remote_copy(
                src_ref=source(peer),
                dst_ref=target.at[me],
                send_sem=sum_send_sem.at[stage],
                recv_sem=sum_recv_sem.at[stage],
                device_id=device(peer),
                device_id_type=MESH,
            ).start()
            return carry

        lax.fori_loop(1, count, step, 0)

    def sum_wait(stage):
        all_bytes(stages[stage][4], sum_recv_sem.at[stage])

    def sum_drain(stage):
        all_bytes(stages[stage][4], sum_send_sem.at[stage])

    def added(target):
        value = target[0].astype(F32)
        for i in range(1, target.shape[0]):
            value = value + target[i].astype(F32)
        return value

    sum_start(0)
    tiles = exchange_wait(4)
    exchange_start(5, "batch", depth_transform(2, tiles))
    pre_halos[1].start()

    spread(1, pg[:C, :])
    sum_wait(0)
    term_send[...] = added(part_recv).astype(BF16)
    sum_start(1)
    spread(2, pg[C:, :])
    for chunk in range(4):
        lanes = pl.ds(chunk * 256, 256)
        act[:, :, lanes] = by_channel_of(act_layers[:, lanes])
    stores = [pltpu.make_async_copy(act, act_out, out_sem.at[0])]
    stores[0].start()

    tiles = exchange_wait(5)
    exchange_start(6, "batch", mix(tiles, unmix_w))

    coef_back[...] = mm(swap[...], tiles).astype(BF16)

    def rows_of(p):
        return pl.ds(p * 16, 16)

    first_half = lax.broadcasted_iota(jnp.int32, (C, 128), 1) < C
    for p in range(KZ):
        product = mm(coef[rows_of(p), :], coef_back[rows_of(p), :], 0, 0)
        mode[p] = jnp.where(first_half, product[:C], product[C:])
    stores.append(pltpu.make_async_copy(mode, mode_out, out_sem.at[1]))
    stores[1].start()

    sum_wait(1)
    full_send[...] = (added(term_recv) * conv_scale).astype(BF16)
    sum_start(2)
    tiles = exchange_wait(6)
    exchange_start(7, "space", depth_transform(3, tiles))

    for copy in pre_halos:
        copy.wait_recv()
    spread(0, jnp.where(me_s > 0, pre_halo[0], jnp.zeros_like(pre_halo[0])))
    spread(3, jnp.where(me_s < G - 1, pre_halo[1], jnp.zeros_like(pre_halo[1])))
    stencil(back_w)
    for phase in range(7):
        exchange_drain(phase)
    for stage in range(2):
        sum_drain(stage)
    for copy in halos + pre_halos:
        copy.wait_send()

    tiles = exchange_wait(7)
    for chunk in range(4):
        lanes = pl.ds(chunk * 256, 256)
        value = (total[:, lanes] + mm(tiles, plane[:, lanes], 0, 0)).astype(BF16)
        grad[:, :, lanes] = by_channel_of(value)
    stores.append(pltpu.make_async_copy(grad, grad_out, out_sem.at[2]))
    stores[2].start()

    sum_wait(2)
    stores.append(pltpu.make_async_copy(full_recv, conv_out, out_sem.at[3]))
    stores[3].start()

    exchange_drain(7)
    sum_drain(2)
    for store in stores:
        store.wait()


def deliver(
    act_in, grad_in, mode_in, conv_in, act_out, grad_out, mode_out, conv_out,
    act, grad, packed_mode, packed_conv, mode, conv, in_sem, out_sem,
):
    held = ((act_in, act), (grad_in, grad), (mode_in, packed_mode), (conv_in, packed_conv))
    loads = [pltpu.make_async_copy(*pair, in_sem.at[i]) for i, pair in enumerate(held)]
    kept = ((act, act_out), (grad, grad_out), (mode, mode_out), (conv, conv_out))
    stores = [pltpu.make_async_copy(*pair, out_sem.at[i]) for i, pair in enumerate(kept)]
    for i in (2, 3, 0, 1):
        loads[i].start()
    loads[2].wait()
    for p in range(KZ):
        mode[p] = packed_mode[p][:, :C]
        mode[KZ + p] = packed_mode[p][:, C:]
    stores[2].start()
    loads[3].wait()
    for i in range(9):
        value = packed_conv[2 * i : 2 * i + 2].reshape(64, 128).astype(F32)
        conv[pl.ds(i * 64, 64), :] = value[:, :C]
        conv[pl.ds(576 + i * 64, 64), :] = value[:, C:]
    for r in range(3):
        value = packed_conv[18 + 3 * r : 21 + 3 * r].reshape(96, 128).astype(F32)
        conv[pl.ds(1152 + r * 192, 96), :] = value[:, :C]
        conv[pl.ds(1152 + r * 192 + 96, 96), :] = value[:, C:]
    stores[3].start()
    for i in (0, 1):
        loads[i].wait()
        stores[i].start()
    for store in stores:
        store.wait()


def shards(snapshots, cotangent, mode_weight, conv_weight):
    plane, depth, swap, inside = make_tables()
    any_space = pl.BlockSpec(memory_space=pltpu.HBM)
    vmem = pltpu.VMEM
    dma = pltpu.SemaphoreType.DMA
    outs = pl.pallas_call(
        kernel,
        name="layer",
        out_shape=(
            jax.ShapeDtypeStruct((C, 2, PLANE), BF16),
            jax.ShapeDtypeStruct((C, 2, PLANE), BF16),
            jax.ShapeDtypeStruct((KZ, C, 128), F32),
            jax.ShapeDtypeStruct((32, 32, 128), BF16),
        ),
        in_specs=[any_space] * 8,
        out_specs=(any_space,) * 4,
        scratch_shapes=[
            vmem((C, 2, PLANE), BF16),
            vmem((C, 2, PLANE), BF16),
            vmem((2 * KZ, C, C), BF16),
            vmem((3, 9, C, C), BF16),
            vmem((256, PLANE), BF16),
            vmem((4, 512, 512), BF16),
            vmem((256, 256), BF16),
            vmem((16, PLANE), BF16),
            vmem((C, 2, PLANE), BF16),
            vmem((C, 2, PLANE), BF16),
            vmem((KZ, C, 128), F32),
            vmem((8, G, 16, 128), BF16),
            vmem((8, G, 16, 128), BF16),
            vmem((2, C, PLANE), BF16),
            vmem((2, C, PLANE), BF16),
            vmem((9 * C, 4 * PLANE), BF16),
            vmem((3 * C, 9 * C), BF16),
            vmem((3 * C, 9 * C), BF16),
            vmem((KZ, 128, 128), BF16),
            vmem((KZ, 128, 128), BF16),
            vmem((128, PLANE), F32),
            vmem((128, PLANE), BF16),
            vmem((128, PLANE), BF16),
            vmem((128, PLANE), BF16),
            vmem((128, PLANE), BF16),
            vmem((256, 128), BF16),
            vmem((256, 128), BF16),
            vmem((1024, 128), BF16),
            vmem((32, 32, 128), BF16),
            vmem((32, 128), BF16),
            vmem((8, 32, 128), BF16),
            vmem((32, 128), BF16),
            vmem((32, 32, 128), BF16),
            dma((8,)),
            dma((4,)),
            dma((8,)),
            dma((8,)),
            dma((2, 4)),
            dma((3,)),
            dma((3,)),
        ],
        compiler_params=pltpu.CompilerParams(
            collective_id=0, has_side_effects=True, vmem_limit_bytes=60 << 20
        ),
    )(
        snapshots[0],
        cotangent[0],
        mode_weight.reshape(2 * KZ, C, C),
        conv_weight.reshape(3, 9, C, C),
        jnp.asarray(plane),
        jnp.asarray(depth),
        jnp.asarray(swap),
        jnp.asarray(inside),
    )
    outs = pl.pallas_call(
        deliver,
        name="deliver",
        out_shape=(
            jax.ShapeDtypeStruct((C, 2, PLANE), BF16),
            jax.ShapeDtypeStruct((C, 2, PLANE), BF16),
            jax.ShapeDtypeStruct((2 * KZ, C, C), F32),
            jax.ShapeDtypeStruct((27 * C, C), F32),
        ),
        in_specs=[any_space] * 4,
        out_specs=(any_space,) * 4,
        scratch_shapes=[vmem(out.shape, out.dtype) for out in outs]
        + [vmem((2 * KZ, C, C), F32), vmem((27 * C, C), F32), dma((4,)), dma((4,))],
        compiler_params=pltpu.CompilerParams(vmem_limit_bytes=60 << 20),
    )(*outs)
    activated, input_gradient, mode_gradient, conv_gradient = outs
    return (
        activated.reshape(1, C, 2, PLANE),
        input_gradient.reshape(1, C, 2, PLANE),
        mode_gradient.reshape(1, 1, 2 * KZ, C, C),
        conv_gradient.reshape(3, 3, 3, C, C),
    )


def solution(mesh):
    in_specs = (
        P("batch", None, "space", None),
        P("batch", None, "space", None),
        P("batch", "space", None, None, None),
        P(),
    )
    out_specs = in_specs
    return jax.shard_map(shards, mesh=mesh, in_specs=in_specs, out_specs=out_specs, check_vma=False)
```

```python
import math

import jax
import jax.numpy as jnp
import ml_dtypes
import numpy as np
from jax import lax
from jax.experimental import pallas as pl
from jax.experimental.pallas import tpu as pltpu
from jax.sharding import PartitionSpec as P

KX = 8
KY = 8
KZ = 12
NX = 32
NY = 32
NZ = 32
PLANE = NX * NY
C = 64
G = 16
SNAPS = 16

MESH = pl.DeviceIdType.MESH
F32 = jnp.float32
BF16 = jnp.bfloat16

inv_root_two = 1.0 / math.sqrt(2.0)
inv_root_two_pi = 1.0 / math.sqrt(2.0 * math.pi)
conv_scale = 1.0 / math.sqrt(SNAPS * NZ * PLANE)


def basis_rows(half_count, length):
    rows = np.arange(2 * half_count)[:, None]
    cells = np.arange(length)[None, :]
    frequency = np.where(rows < half_count, rows, rows - half_count + 1)
    phases = ((frequency * cells) % length).astype(np.float32) * np.float32(2.0 * math.pi / length)
    return np.where(rows < half_count, np.cos(phases), np.sin(phases)).astype(np.float32)


def make_tables():
    across = basis_rows(KX, NX)
    along_y = basis_rows(KY, NY)
    depth_rows = basis_rows(KZ, NZ)
    outer = across[None, :, :, None] * along_y[:, None, None, :]
    plane = (outer.reshape(256, PLANE) * np.float32(2.0 / math.sqrt(PLANE))).astype(ml_dtypes.bfloat16)
    analysis = (depth_rows * np.float32(math.sqrt(2.0 / NZ))).astype(ml_dtypes.bfloat16)
    synthesis = (depth_rows.T * np.float32(math.sqrt(2.0 / (2 * KZ)))).astype(ml_dtypes.bfloat16)
    to_modes = np.zeros((2, G, 16, 2, G, 16), ml_dtypes.bfloat16)
    to_cells = np.zeros((2, G, 16, 2, G, 16), ml_dtypes.bfloat16)
    down = analysis.reshape(2, KZ, 16, 2).transpose(0, 1, 3, 2)
    up = synthesis.reshape(16, 2, 2, KZ).transpose(1, 0, 2, 3)
    for mode in range(16):
        to_modes[:, mode, :KZ, :, :, mode] = down
        to_cells[:, :, mode, :, mode, :KZ] = up
    to_modes = to_modes.reshape(512, 512)
    to_cells = to_cells.reshape(512, 512)
    depth = np.stack([to_modes, to_cells, to_cells.T, to_modes.T])
    swap = np.zeros((16, 16, 16, 16), ml_dtypes.bfloat16)
    for a in range(16):
        for b in range(16):
            swap[a, b, b, a] = 1
    x = np.arange(PLANE) // NY
    y = np.arange(PLANE) % NY
    inside = np.zeros((16, PLANE), ml_dtypes.bfloat16)
    for tap in range(9):
        dx, dy = tap // 3 - 1, tap % 3 - 1
        inside[tap] = (x + dx >= 0) & (x + dx < NX) & (y + dy >= 0) & (y + dy < NY)
    return plane, depth, swap.reshape(256, 256), inside


def mm(left, right, left_dim=1, right_dim=0):
    return lax.dot_general(
        left, right, (((left_dim,), (right_dim,)), ((), ())), preferred_element_type=F32
    )


def kernel(
    x_in, cot_in, w_in, cw_in, plane_in, depth_in, swap_in, inside_in,
    act_out, grad_out, mode_out, conv_out,
    x, cot, w, cw, plane, depth, swap, inside,
    act, grad, mode,
    send, recv, halo, pre_halo, cols, forward_w, back_w, mix_w, unmix_w, total, pg, layers, cot_layers, act_layers, coef, coef_back,
    part_send, part_recv, term_send, term_recv, full_send, full_recv,
    in_sem, out_sem, send_sem, recv_sem, halo_sem, sum_send_sem, sum_recv_sem,
):
    me_b = lax.axis_index("batch")
    me_s = lax.axis_index("space")
    mine = {"batch": me_b, "space": me_s}
    beside = me_s - me_s % 2

    barrier = pltpu.get_barrier_semaphore()
    for step in (8, 7, 9, 6, 10, 5, 11, 4, 12, 3, 13, 2, 14, 1, 15):
        peer_b, peer_s = lax.rem(me_b + step, G), lax.rem(me_s + step, G)
        for target in (
            {"space": peer_s}, {"batch": peer_b}, {"batch": peer_b, "space": beside + 1 - me_s % 2},
        ):
            pl.semaphore_signal(barrier, inc=1, device_id=target, device_id_type=MESH)

    loads = [
        pltpu.make_async_copy(source, target, in_sem.at[i])
        for i, (source, target) in enumerate(
            (
                (x_in, x), (plane_in, plane), (depth_in, depth), (inside_in, inside),
                (cw_in, cw), (swap_in, swap), (w_in, w), (cot_in, cot),
            )
        )
    ]
    for load in loads:
        load.start()

    def peers_of(axis):
        if axis == "space":
            order = [(z, y) for z in (4, 3, 5, 2, 6, 1, 7, 0) for y in (1, 0)][:-1]
            return [lax.rem(me_s // 2 + z, 8) * 2 + lax.rem(me_s + y, 2) for z, y in order]
        order = [(x, y, c) for y in (1, 0) for x in (2, 1, 3, 0) for c in (1, 0)][:-1]
        return [
            lax.rem(me_b // 4 + x, 4) * 4 + lax.rem(me_b // 2 + y, 2) * 2 + lax.rem(me_b + c, 2)
            for x, y, c in order
        ]

    partners = {axis: peers_of(axis) for axis in ("space", "batch")}

    def tile_copy(phase, axis, source, slot):
        return pltpu.make_async_remote_copy(
            src_ref=send.at[phase, source],
            dst_ref=recv.at[phase, slot],
            send_sem=send_sem.at[phase],
            recv_sem=recv_sem.at[phase],
            device_id={axis: source},
            device_id_type=MESH,
        )

    def exchange_start(phase, axis, value):
        me = mine[axis]
        send[phase] = value.reshape(G, 16, 128)

        for peer in partners[axis]:
            tile_copy(phase, axis, peer, me).start()
        recv[phase, me] = send[phase, me]

    def all_bytes(buffer, sem):
        others = buffer.at[pl.ds(0, buffer.shape[0] - 1)]
        pltpu.make_async_copy(others, others, sem).wait()

    def exchange_wait(phase):
        all_bytes(recv.at[phase], recv_sem.at[phase])
        return recv[phase].reshape(256, 128)

    def exchange_drain(phase):
        all_bytes(send.at[phase], send_sem.at[phase])

    def halo_copy(source, target, slot, which, offset):
        return pltpu.make_async_remote_copy(
            src_ref=source,
            dst_ref=target.at[slot],
            send_sem=halo_sem.at[0, which],
            recv_sem=halo_sem.at[1, which],
            device_id={"space": lax.rem(me_s + offset, G)},
            device_id_type=MESH,
        )

    def depth_transform(which, tiles):
        stacked = jnp.concatenate([tiles[:, :C], tiles[:, C:]], axis=0)
        both = mm(depth[which], stacked)
        return jnp.concatenate([both[:256], both[256:]], axis=1).astype(BF16)

    def spread(layer, cells):
        for tap in range(9):
            shift = (tap // 3 - 1) * NY + (tap % 3 - 1)
            moved = cells
            if shift:
                moved = pltpu.roll(cells, (-shift) % PLANE, 1) * inside[tap : tap + 1, :]
            cols[tap * C : (tap + 1) * C, layer * PLANE : (layer + 1) * PLANE] = moved

    def stencil(weights):
        width = 256
        for chunk in range(PLANE // width):
            lanes = [pl.ds(layer * PLANE + chunk * width, width) for layer in range(4)]
            acc = mm(weights[C : 3 * C, :], cols[:, lanes[1]])
            acc = acc + mm(weights[0 : 2 * C, :], cols[:, lanes[2]])
            first = mm(weights[2 * C : 3 * C, :], cols[:, lanes[0]])
            last = mm(weights[0:C, :], cols[:, lanes[3]])
            total[:, pl.ds(chunk * width, width)] = acc + jnp.concatenate([first, last], axis=0)

    row = lax.broadcasted_iota(jnp.int32, (128, 128), 0)
    column = lax.broadcasted_iota(jnp.int32, (128, 128), 1)
    split = jnp.where(column == lax.rem(row, C) * 2 + row // C, 1.0, 0.0).astype(BF16)

    def by_layer_of(ref):
        return mm(split, ref[...].reshape(128, PLANE)).astype(BF16)

    def by_channel_of(value):
        return mm(split, value, 0, 0).astype(BF16).reshape(C, 2, value.shape[1])

    loads[0].wait()
    loads[1].wait()
    layers[...] = by_layer_of(x)
    plane_coef = mm(plane[...], layers[...], 1, 1).astype(BF16)
    pl.semaphore_wait(barrier, 3 * (G - 1))
    exchange_start(0, "space", plane_coef)
    halos = [
        halo_copy(layers.at[pl.ds(C, C), :], halo, 0, 0, 1),
        halo_copy(layers.at[pl.ds(0, C), :], halo, 1, 1, G - 1),
    ]
    halos[0].start()

    loads[2].wait()
    loads[3].wait()
    spread(1, layers[:C, :])
    tiles = exchange_wait(0)
    exchange_start(1, "batch", depth_transform(0, tiles))
    halos[1].start()

    loads[4].wait()
    for a in range(3):
        for tap in range(9):
            block = cw[a, tap]
            forward_w[(2 - a) * C : (3 - a) * C, tap * C : (tap + 1) * C] = (
                block.astype(F32).T.astype(BF16)
            )
            back_w[a * C : (a + 1) * C, (8 - tap) * C : (9 - tap) * C] = block
    loads[5].wait()
    loads[6].wait()
    mix_w[...] = jnp.zeros_like(mix_w)
    for p in range(KZ):
        mix_w[p, :C, :C] = w[p]
        mix_w[p, C:, C:] = w[KZ + p]

    z_mode = lax.broadcasted_iota(jnp.int32, (256, 128), 0) % 16

    def mix(tiles, weights):
        picked = [
            tiles * jnp.where(z_mode == p, 1.0, 0.0).astype(BF16) for p in range(KZ)
        ]
        return mm(jnp.concatenate(picked, axis=1), weights[...].reshape(KZ * 128, 128)).astype(BF16)

    tiles = exchange_wait(1)
    exchange_start(2, "batch", mix(tiles, mix_w))
    coef[...] = mm(swap[...], tiles).astype(BF16)
    for p in range(KZ):
        unmix_w[p] = mix_w[p].astype(F32).T.astype(BF16)

    spread(2, layers[C:, :])
    for copy in halos:
        copy.wait_recv()
    spread(0, jnp.where(me_s > 0, halo[0], jnp.zeros_like(halo[0])))
    spread(3, jnp.where(me_s < G - 1, halo[1], jnp.zeros_like(halo[1])))

    tiles = exchange_wait(2)
    exchange_start(3, "space", depth_transform(1, tiles))
    stencil(forward_w)
    loads[7].wait()
    cot_layers[...] = by_layer_of(cot)
    tiles = exchange_wait(3)
    doubled = tiles * jnp.asarray(2.0, BF16)

    for chunk in range(4):
        lanes = pl.ds(chunk * 256, 256)
        total[:, lanes] += mm(doubled, plane[:, lanes], 0, 0)
    for layer in range(2):
        for chunk in range(4):
            lanes = pl.ds(chunk * 256, 256)
            rows = pl.ds(layer * C, C)
            pre = total[rows, lanes]
            normal_cdf = 0.5 * (1.0 + lax.erf(pre * inv_root_two))
            density = jnp.exp(-0.5 * pre * pre) * inv_root_two_pi
            act_layers[rows, lanes] = (pre * normal_cdf).astype(BF16)
            pg[rows, lanes] = (
                cot_layers[rows, lanes].astype(F32) * (normal_cdf + pre * density)
            ).astype(BF16)
    back_plane = (mm(plane[...], pg[...], 1, 1) * 2.0).astype(BF16)
    exchange_start(4, "space", back_plane)
    pre_halos = [
        halo_copy(pg.at[pl.ds(C, C), :], pre_halo, 0, 2, 1),
        halo_copy(pg.at[pl.ds(0, C), :], pre_halo, 1, 3, G - 1),
    ]
    pre_halos[0].start()

    for r in range(3):
        rows = pl.ds(r * 192, 192)
        by_layer = [
            mm(cols[rows, pl.ds(layer * PLANE, PLANE)], pg[...], 1, 1) for layer in range(4)
        ]
        terms = [by_layer[a][:, :C] + by_layer[a + 1][:, C:] for a in range(3)]
        part_send[rows, :] = jnp.concatenate(terms[:2], axis=1).astype(BF16)
        part_send[pl.ds(576 + r * 96, 96), :] = jnp.concatenate(
            [terms[2][:96], terms[2][96:]], axis=1
        ).astype(BF16)
    part_send[pl.ds(864, 160), :] = jnp.zeros((160, 128), BF16)

    def part_rows(i):
        return part_send.at[pl.ds(pl.multiple_of(i * 32, 32), 32), :]

    def in_layer(i):
        return {"batch": i // 2, "space": beside + i % 2}

    def in_column(i):
        return {"space": i * 2 + me_s % 2}

    at_layer = me_b * 2 + me_s % 2
    stages = (
        (32, at_layer, in_layer, part_rows, part_recv),
        (8, me_s // 2, in_column, lambda i: term_send, term_recv),
        (32, at_layer, in_layer, lambda i: full_send, full_recv),
    )

    def sum_start(stage):
        count, me, device, source, target = stages[stage]
        target[me] = source(me)[...]

        def step(i, carry):
            peer = lax.rem(me + i, count)
            pltpu.make_async_remote_copy(
                src_ref=source(peer),
                dst_ref=target.at[me],
                send_sem=sum_send_sem.at[stage],
                recv_sem=sum_recv_sem.at[stage],
                device_id=device(peer),
                device_id_type=MESH,
            ).start()
            return carry

        lax.fori_loop(1, count, step, 0)

    def sum_wait(stage):
        all_bytes(stages[stage][4], sum_recv_sem.at[stage])

    def sum_drain(stage):
        all_bytes(stages[stage][4], sum_send_sem.at[stage])

    def added(target):
        value = target[0].astype(F32)
        for i in range(1, target.shape[0]):
            value = value + target[i].astype(F32)
        return value

    sum_start(0)
    tiles = exchange_wait(4)
    exchange_start(5, "batch", depth_transform(2, tiles))
    pre_halos[1].start()

    spread(1, pg[:C, :])
    sum_wait(0)
    term_send[...] = added(part_recv).astype(BF16)
    sum_start(1)
    spread(2, pg[C:, :])
    for chunk in range(4):
        lanes = pl.ds(chunk * 256, 256)
        act[:, :, lanes] = by_channel_of(act_layers[:, lanes])
    stores = [pltpu.make_async_copy(act, act_out, out_sem.at[0])]
    stores[0].start()

    tiles = exchange_wait(5)
    exchange_start(6, "batch", mix(tiles, unmix_w))

    coef_back[...] = mm(swap[...], tiles).astype(BF16)

    def rows_of(p):
        return pl.ds(p * 16, 16)

    first_half = lax.broadcasted_iota(jnp.int32, (C, 128), 1) < C
    for p in range(KZ):
        product = mm(coef[rows_of(p), :], coef_back[rows_of(p), :], 0, 0)
        mode[p] = jnp.where(first_half, product[:C], product[C:])
    stores.append(pltpu.make_async_copy(mode, mode_out, out_sem.at[1]))
    stores[1].start()

    sum_wait(1)
    full_send[...] = (added(term_recv) * conv_scale).astype(BF16)
    sum_start(2)
    tiles = exchange_wait(6)
    exchange_start(7, "space", depth_transform(3, tiles))

    for copy in pre_halos:
        copy.wait_recv()
    spread(0, jnp.where(me_s > 0, pre_halo[0], jnp.zeros_like(pre_halo[0])))
    spread(3, jnp.where(me_s < G - 1, pre_halo[1], jnp.zeros_like(pre_halo[1])))
    stencil(back_w)
    for phase in range(7):
        exchange_drain(phase)
    for stage in range(2):
        sum_drain(stage)
    for copy in halos + pre_halos:
        copy.wait_send()

    tiles = exchange_wait(7)
    for chunk in range(4):
        lanes = pl.ds(chunk * 256, 256)
        value = (total[:, lanes] + mm(tiles, plane[:, lanes], 0, 0)).astype(BF16)
        grad[:, :, lanes] = by_channel_of(value)
    stores.append(pltpu.make_async_copy(grad, grad_out, out_sem.at[2]))
    stores[2].start()

    sum_wait(2)
    stores.append(pltpu.make_async_copy(full_recv, conv_out, out_sem.at[3]))
    stores[3].start()

    exchange_drain(7)
    sum_drain(2)
    for store in stores:
        store.wait()


def deliver(
    act_in, grad_in, mode_in, conv_in, act_out, grad_out, mode_out, conv_out,
    act, grad, packed_mode, packed_conv, mode, conv, in_sem, out_sem,
):
    held = ((act_in, act), (grad_in, grad), (mode_in, packed_mode), (conv_in, packed_conv))
    loads = [pltpu.make_async_copy(*pair, in_sem.at[i]) for i, pair in enumerate(held)]
    kept = ((act, act_out), (grad, grad_out), (mode, mode_out), (conv, conv_out))
    stores = [pltpu.make_async_copy(*pair, out_sem.at[i]) for i, pair in enumerate(kept)]
    for i in (2, 3, 0, 1):
        loads[i].start()
    loads[2].wait()
    for p in range(KZ):
        mode[p] = packed_mode[p][:, :C]
        mode[KZ + p] = packed_mode[p][:, C:]
    stores[2].start()
    loads[3].wait()
    for i in range(9):
        value = packed_conv[2 * i : 2 * i + 2].reshape(64, 128).astype(F32)
        conv[pl.ds(i * 64, 64), :] = value[:, :C]
        conv[pl.ds(576 + i * 64, 64), :] = value[:, C:]
    for r in range(3):
        value = packed_conv[18 + 3 * r : 21 + 3 * r].reshape(96, 128).astype(F32)
        conv[pl.ds(1152 + r * 192, 96), :] = value[:, :C]
        conv[pl.ds(1152 + r * 192 + 96, 96), :] = value[:, C:]
    stores[3].start()
    for i in (0, 1):
        loads[i].wait()
        stores[i].start()
    for store in stores:
        store.wait()


def shards(snapshots, cotangent, mode_weight, conv_weight):
    plane, depth, swap, inside = make_tables()
    any_space = pl.BlockSpec(memory_space=pltpu.HBM)
    vmem = pltpu.VMEM
    dma = pltpu.SemaphoreType.DMA
    outs = pl.pallas_call(
        kernel,
        name="layer",
        out_shape=(
            jax.ShapeDtypeStruct((C, 2, PLANE), BF16),
            jax.ShapeDtypeStruct((C, 2, PLANE), BF16),
            jax.ShapeDtypeStruct((KZ, C, 128), F32),
            jax.ShapeDtypeStruct((32, 32, 128), BF16),
        ),
        in_specs=[any_space] * 8,
        out_specs=(any_space,) * 4,
        scratch_shapes=[
            vmem((C, 2, PLANE), BF16),
            vmem((C, 2, PLANE), BF16),
            vmem((2 * KZ, C, C), BF16),
            vmem((3, 9, C, C), BF16),
            vmem((256, PLANE), BF16),
            vmem((4, 512, 512), BF16),
            vmem((256, 256), BF16),
            vmem((16, PLANE), BF16),
            vmem((C, 2, PLANE), BF16),
            vmem((C, 2, PLANE), BF16),
            vmem((KZ, C, 128), F32),
            vmem((8, G, 16, 128), BF16),
            vmem((8, G, 16, 128), BF16),
            vmem((2, C, PLANE), BF16),
            vmem((2, C, PLANE), BF16),
            vmem((9 * C, 4 * PLANE), BF16),
            vmem((3 * C, 9 * C), BF16),
            vmem((3 * C, 9 * C), BF16),
            vmem((KZ, 128, 128), BF16),
            vmem((KZ, 128, 128), BF16),
            vmem((128, PLANE), F32),
            vmem((128, PLANE), BF16),
            vmem((128, PLANE), BF16),
            vmem((128, PLANE), BF16),
            vmem((128, PLANE), BF16),
            vmem((256, 128), BF16),
            vmem((256, 128), BF16),
            vmem((1024, 128), BF16),
            vmem((32, 32, 128), BF16),
            vmem((32, 128), BF16),
            vmem((8, 32, 128), BF16),
            vmem((32, 128), BF16),
            vmem((32, 32, 128), BF16),
            dma((8,)),
            dma((4,)),
            dma((8,)),
            dma((8,)),
            dma((2, 4)),
            dma((3,)),
            dma((3,)),
        ],
        compiler_params=pltpu.CompilerParams(
            collective_id=0, has_side_effects=True, vmem_limit_bytes=60 << 20
        ),
    )(
        snapshots[0],
        cotangent[0],
        mode_weight.reshape(2 * KZ, C, C),
        conv_weight.reshape(3, 9, C, C),
        jnp.asarray(plane),
        jnp.asarray(depth),
        jnp.asarray(swap),
        jnp.asarray(inside),
    )
    outs = pl.pallas_call(
        deliver,
        name="deliver",
        out_shape=(
            jax.ShapeDtypeStruct((C, 2, PLANE), BF16),
            jax.ShapeDtypeStruct((C, 2, PLANE), BF16),
            jax.ShapeDtypeStruct((2 * KZ, C, C), F32),
            jax.ShapeDtypeStruct((27 * C, C), F32),
        ),
        in_specs=[any_space] * 4,
        out_specs=(any_space,) * 4,
        scratch_shapes=[vmem(out.shape, out.dtype) for out in outs]
        + [vmem((2 * KZ, C, C), F32), vmem((27 * C, C), F32), dma((4,)), dma((4,))],
        compiler_params=pltpu.CompilerParams(vmem_limit_bytes=60 << 20),
    )(*outs)
    activated, input_gradient, mode_gradient, conv_gradient = outs
    return (
        activated.reshape(1, C, 2, PLANE),
        input_gradient.reshape(1, C, 2, PLANE),
        mode_gradient.reshape(1, 1, 2 * KZ, C, C),
        conv_gradient.reshape(3, 3, 3, C, C),
    )


def solution(mesh):
    in_specs = (
        P("batch", None, "space", None),
        P("batch", None, "space", None),
        P("batch", "space", None, None, None),
        P(),
    )
    out_specs = in_specs
    return jax.shard_map(shards, mesh=mesh, in_specs=in_specs, out_specs=out_specs, check_vma=False)
```

```python
import math

import jax
import jax.numpy as jnp
import ml_dtypes
import numpy as np
from jax import lax
from jax.experimental import pallas as pl
from jax.experimental.pallas import tpu as pltpu
from jax.sharding import PartitionSpec as P

KX = 8
KY = 8
KZ = 12
NX = 32
NY = 32
NZ = 32
PLANE = NX * NY
C = 64
G = 16
SNAPS = 16

MESH = pl.DeviceIdType.MESH
F32 = jnp.float32
BF16 = jnp.bfloat16

inv_root_two = 1.0 / math.sqrt(2.0)
inv_root_two_pi = 1.0 / math.sqrt(2.0 * math.pi)
conv_scale = 1.0 / math.sqrt(SNAPS * NZ * PLANE)


def basis_rows(half_count, length):
    rows = np.arange(2 * half_count)[:, None]
    cells = np.arange(length)[None, :]
    frequency = np.where(rows < half_count, rows, rows - half_count + 1)
    phases = ((frequency * cells) % length).astype(np.float32) * np.float32(2.0 * math.pi / length)
    return np.where(rows < half_count, np.cos(phases), np.sin(phases)).astype(np.float32)


def make_tables():
    across = basis_rows(KX, NX)
    along_y = basis_rows(KY, NY)
    depth_rows = basis_rows(KZ, NZ)
    outer = across[None, :, :, None] * along_y[:, None, None, :]
    plane = (outer.reshape(256, PLANE) * np.float32(2.0 / math.sqrt(PLANE))).astype(ml_dtypes.bfloat16)
    analysis = (depth_rows * np.float32(math.sqrt(2.0 / NZ))).astype(ml_dtypes.bfloat16)
    synthesis = (depth_rows.T * np.float32(math.sqrt(2.0 / (2 * KZ)))).astype(ml_dtypes.bfloat16)
    to_modes = np.zeros((2, G, 16, 2, G, 16), ml_dtypes.bfloat16)
    to_cells = np.zeros((2, G, 16, 2, G, 16), ml_dtypes.bfloat16)
    down = analysis.reshape(2, KZ, 16, 2).transpose(0, 1, 3, 2)
    up = synthesis.reshape(16, 2, 2, KZ).transpose(1, 0, 2, 3)
    for mode in range(16):
        to_modes[:, mode, :KZ, :, :, mode] = down
        to_cells[:, :, mode, :, mode, :KZ] = up
    to_modes = to_modes.reshape(512, 512)
    to_cells = to_cells.reshape(512, 512)
    depth = np.stack([to_modes, to_cells, to_cells.T, to_modes.T])
    swap = np.zeros((16, 16, 16, 16), ml_dtypes.bfloat16)
    for a in range(16):
        for b in range(16):
            swap[a, b, b, a] = 1
    x = np.arange(PLANE) // NY
    y = np.arange(PLANE) % NY
    inside = np.zeros((16, PLANE), ml_dtypes.bfloat16)
    for tap in range(9):
        dx, dy = tap // 3 - 1, tap % 3 - 1
        inside[tap] = (x + dx >= 0) & (x + dx < NX) & (y + dy >= 0) & (y + dy < NY)
    return plane, depth, swap.reshape(256, 256), inside


def mm(left, right, left_dim=1, right_dim=0):
    return lax.dot_general(
        left, right, (((left_dim,), (right_dim,)), ((), ())), preferred_element_type=F32
    )


def kernel(
    x_in, cot_in, w_in, cw_in, plane_in, depth_in, swap_in, inside_in,
    act_out, grad_out, mode_out, conv_out,
    x, cot, w, cw, plane, depth, swap, inside,
    act, grad, mode,
    send, recv, halo, pre_halo, cols, forward_w, back_w, mix_w, unmix_w, total, pg, layers, cot_layers, act_layers, coef, coef_back,
    part_send, part_recv, term_send, term_recv, full_send, full_recv,
    in_sem, out_sem, send_sem, recv_sem, halo_sem, sum_send_sem, sum_recv_sem,
):
    me_b = lax.axis_index("batch")
    me_s = lax.axis_index("space")
    mine = {"batch": me_b, "space": me_s}
    beside = me_s - me_s % 2

    barrier = pltpu.get_barrier_semaphore()
    for step in (8, 7, 9, 6, 10, 5, 11, 4, 12, 3, 13, 2, 14, 1, 15):
        peer_b, peer_s = lax.rem(me_b + step, G), lax.rem(me_s + step, G)
        for target in (
            {"space": peer_s}, {"batch": peer_b}, {"batch": peer_b, "space": beside + 1 - me_s % 2},
        ):
            pl.semaphore_signal(barrier, inc=1, device_id=target, device_id_type=MESH)

    loads = [
        pltpu.make_async_copy(source, target, in_sem.at[i])
        for i, (source, target) in enumerate(
            (
                (x_in, x), (plane_in, plane), (depth_in, depth), (inside_in, inside),
                (cw_in, cw), (swap_in, swap), (w_in, w), (cot_in, cot),
            )
        )
    ]
    for load in loads:
        load.start()

    def peers_of(axis):
        if axis == "space":
            order = [(z, y) for z in (4, 3, 5, 2, 6, 1, 7, 0) for y in (1, 0)][:-1]
            return [lax.rem(me_s // 2 + z, 8) * 2 + lax.rem(me_s + y, 2) for z, y in order]
        order = [(x, y, c) for y in (1, 0) for x in (2, 1, 3, 0) for c in (1, 0)][:-1]
        return [
            lax.rem(me_b // 4 + x, 4) * 4 + lax.rem(me_b // 2 + y, 2) * 2 + lax.rem(me_b + c, 2)
            for x, y, c in order
        ]

    partners = {axis: peers_of(axis) for axis in ("space", "batch")}

    def tile_copy(phase, axis, source, slot):
        return pltpu.make_async_remote_copy(
            src_ref=send.at[phase, source],
            dst_ref=recv.at[phase, slot],
            send_sem=send_sem.at[phase],
            recv_sem=recv_sem.at[phase],
            device_id={axis: source},
            device_id_type=MESH,
        )

    def exchange_start(phase, axis, value):
        me = mine[axis]
        send[phase] = value.reshape(G, 16, 128)

        for peer in partners[axis]:
            tile_copy(phase, axis, peer, me).start()
        recv[phase, me] = send[phase, me]

    def all_bytes(buffer, sem):
        others = buffer.at[pl.ds(0, buffer.shape[0] - 1)]
        pltpu.make_async_copy(others, others, sem).wait()

    def exchange_wait(phase):
        all_bytes(recv.at[phase], recv_sem.at[phase])
        return recv[phase].reshape(256, 128)

    def exchange_drain(phase):
        all_bytes(send.at[phase], send_sem.at[phase])

    def halo_copy(source, target, slot, which, offset):
        return pltpu.make_async_remote_copy(
            src_ref=source,
            dst_ref=target.at[slot],
            send_sem=halo_sem.at[0, which],
            recv_sem=halo_sem.at[1, which],
            device_id={"space": lax.rem(me_s + offset, G)},
            device_id_type=MESH,
        )

    def depth_transform(which, tiles):
        stacked = jnp.concatenate([tiles[:, :C], tiles[:, C:]], axis=0)
        both = mm(depth[which], stacked)
        return jnp.concatenate([both[:256], both[256:]], axis=1).astype(BF16)

    def spread(layer, cells):
        for tap in range(9):
            shift = (tap // 3 - 1) * NY + (tap % 3 - 1)
            moved = cells
            if shift:
                moved = pltpu.roll(cells, (-shift) % PLANE, 1) * inside[tap : tap + 1, :]
            cols[tap * C : (tap + 1) * C, layer * PLANE : (layer + 1) * PLANE] = moved

    def stencil(weights):
        width = 256
        for chunk in range(PLANE // width):
            lanes = [pl.ds(layer * PLANE + chunk * width, width) for layer in range(4)]
            acc = mm(weights[C : 3 * C, :], cols[:, lanes[1]])
            acc = acc + mm(weights[0 : 2 * C, :], cols[:, lanes[2]])
            first = mm(weights[2 * C : 3 * C, :], cols[:, lanes[0]])
            last = mm(weights[0:C, :], cols[:, lanes[3]])
            total[:, pl.ds(chunk * width, width)] = acc + jnp.concatenate([first, last], axis=0)

    row = lax.broadcasted_iota(jnp.int32, (128, 128), 0)
    column = lax.broadcasted_iota(jnp.int32, (128, 128), 1)
    split = jnp.where(column == lax.rem(row, C) * 2 + row // C, 1.0, 0.0).astype(BF16)

    def by_layer_of(ref):
        return mm(split, ref[...].reshape(128, PLANE)).astype(BF16)

    def by_channel_of(value):
        return mm(split, value, 0, 0).astype(BF16).reshape(C, 2, value.shape[1])

    loads[0].wait()
    loads[1].wait()
    layers[...] = by_layer_of(x)
    plane_coef = mm(plane[...], layers[...], 1, 1).astype(BF16)
    pl.semaphore_wait(barrier, 3 * (G - 1))
    exchange_start(0, "space", plane_coef)
    halos = [
        halo_copy(layers.at[pl.ds(C, C), :], halo, 0, 0, 1),
        halo_copy(layers.at[pl.ds(0, C), :], halo, 1, 1, G - 1),
    ]
    halos[0].start()

    loads[2].wait()
    loads[3].wait()
    spread(1, layers[:C, :])
    tiles = exchange_wait(0)
    exchange_start(1, "batch", depth_transform(0, tiles))
    halos[1].start()

    loads[4].wait()
    for a in range(3):
        for tap in range(9):
            block = cw[a, tap]
            forward_w[(2 - a) * C : (3 - a) * C, tap * C : (tap + 1) * C] = (
                block.astype(F32).T.astype(BF16)
            )
            back_w[a * C : (a + 1) * C, (8 - tap) * C : (9 - tap) * C] = block
    loads[5].wait()
    loads[6].wait()
    mix_w[...] = jnp.zeros_like(mix_w)
    for p in range(KZ):
        mix_w[p, :C, :C] = w[p]
        mix_w[p, C:, C:] = w[KZ + p]

    z_mode = lax.broadcasted_iota(jnp.int32, (256, 128), 0) % 16

    def mix(tiles, weights):
        picked = [
            tiles * jnp.where(z_mode == p, 1.0, 0.0).astype(BF16) for p in range(KZ)
        ]
        return mm(jnp.concatenate(picked, axis=1), weights[...].reshape(KZ * 128, 128)).astype(BF16)

    tiles = exchange_wait(1)
    exchange_start(2, "batch", mix(tiles, mix_w))
    coef[...] = mm(swap[...], tiles).astype(BF16)
    for p in range(KZ):
        unmix_w[p] = mix_w[p].astype(F32).T.astype(BF16)

    spread(2, layers[C:, :])
    for copy in halos:
        copy.wait_recv()
    spread(0, jnp.where(me_s > 0, halo[0], jnp.zeros_like(halo[0])))
    spread(3, jnp.where(me_s < G - 1, halo[1], jnp.zeros_like(halo[1])))

    tiles = exchange_wait(2)
    exchange_start(3, "space", depth_transform(1, tiles))
    stencil(forward_w)
    loads[7].wait()
    cot_layers[...] = by_layer_of(cot)
    tiles = exchange_wait(3)
    doubled = tiles * jnp.asarray(2.0, BF16)

    for chunk in range(4):
        lanes = pl.ds(chunk * 256, 256)
        total[:, lanes] += mm(doubled, plane[:, lanes], 0, 0)
    for layer in range(2):
        for chunk in range(4):
            lanes = pl.ds(chunk * 256, 256)
            rows = pl.ds(layer * C, C)
            pre = total[rows, lanes]
            normal_cdf = 0.5 * (1.0 + lax.erf(pre * inv_root_two))
            density = jnp.exp(-0.5 * pre * pre) * inv_root_two_pi
            act_layers[rows, lanes] = (pre * normal_cdf).astype(BF16)
            pg[rows, lanes] = (
                cot_layers[rows, lanes].astype(F32) * (normal_cdf + pre * density)
            ).astype(BF16)
    back_plane = (mm(plane[...], pg[...], 1, 1) * 2.0).astype(BF16)
    exchange_start(4, "space", back_plane)
    pre_halos = [
        halo_copy(pg.at[pl.ds(C, C), :], pre_halo, 0, 2, 1),
        halo_copy(pg.at[pl.ds(0, C), :], pre_halo, 1, 3, G - 1),
    ]
    pre_halos[0].start()

    for r in range(3):
        rows = pl.ds(r * 192, 192)
        by_layer = [
            mm(cols[rows, pl.ds(layer * PLANE, PLANE)], pg[...], 1, 1) for layer in range(4)
        ]
        terms = [by_layer[a][:, :C] + by_layer[a + 1][:, C:] for a in range(3)]
        part_send[rows, :] = jnp.concatenate(terms[:2], axis=1).astype(BF16)
        part_send[pl.ds(576 + r * 96, 96), :] = jnp.concatenate(
            [terms[2][:96], terms[2][96:]], axis=1
        ).astype(BF16)
    part_send[pl.ds(864, 160), :] = jnp.zeros((160, 128), BF16)

    def part_rows(i):
        return part_send.at[pl.ds(pl.multiple_of(i * 32, 32), 32), :]

    def in_layer(i):
        return {"batch": i // 2, "space": beside + i % 2}

    def in_column(i):
        return {"space": i * 2 + me_s % 2}

    at_layer = me_b * 2 + me_s % 2
    stages = (
        (32, at_layer, in_layer, part_rows, part_recv),
        (8, me_s // 2, in_column, lambda i: term_send, term_recv),
        (32, at_layer, in_layer, lambda i: full_send, full_recv),
    )

    def sum_start(stage):
        count, me, device, source, target = stages[stage]
        target[me] = source(me)[...]

        for i in sorted(range(1, count), key=lambda i: -min(i, count - i)):
            peer = lax.rem(me + i, count)
            pltpu.make_async_remote_copy(
                src_ref=source(peer),
                dst_ref=target.at[me],
                send_sem=sum_send_sem.at[stage],
                recv_sem=sum_recv_sem.at[stage],
                device_id=device(peer),
                device_id_type=MESH,
            ).start()

    def sum_wait(stage):
        all_bytes(stages[stage][4], sum_recv_sem.at[stage])

    def sum_drain(stage):
        all_bytes(stages[stage][4], sum_send_sem.at[stage])

    def added(target):
        value = target[0].astype(F32)
        for i in range(1, target.shape[0]):
            value = value + target[i].astype(F32)
        return value

    sum_start(0)
    tiles = exchange_wait(4)
    exchange_start(5, "batch", depth_transform(2, tiles))
    pre_halos[1].start()

    spread(1, pg[:C, :])
    sum_wait(0)
    term_send[...] = added(part_recv).astype(BF16)
    sum_start(1)
    spread(2, pg[C:, :])
    for chunk in range(4):
        lanes = pl.ds(chunk * 256, 256)
        act[:, :, lanes] = by_channel_of(act_layers[:, lanes])
    stores = [pltpu.make_async_copy(act, act_out, out_sem.at[0])]
    stores[0].start()

    tiles = exchange_wait(5)
    exchange_start(6, "batch", mix(tiles, unmix_w))

    coef_back[...] = mm(swap[...], tiles).astype(BF16)

    def rows_of(p):
        return pl.ds(p * 16, 16)

    first_half = lax.broadcasted_iota(jnp.int32, (C, 128), 1) < C
    for p in range(KZ):
        product = mm(coef[rows_of(p), :], coef_back[rows_of(p), :], 0, 0)
        mode[p] = jnp.where(first_half, product[:C], product[C:])
    stores.append(pltpu.make_async_copy(mode, mode_out, out_sem.at[1]))
    stores[1].start()

    sum_wait(1)
    full_send[...] = (added(term_recv) * conv_scale).astype(BF16)
    sum_start(2)
    tiles = exchange_wait(6)
    exchange_start(7, "space", depth_transform(3, tiles))

    for copy in pre_halos:
        copy.wait_recv()
    spread(0, jnp.where(me_s > 0, pre_halo[0], jnp.zeros_like(pre_halo[0])))
    spread(3, jnp.where(me_s < G - 1, pre_halo[1], jnp.zeros_like(pre_halo[1])))
    stencil(back_w)
    for phase in range(7):
        exchange_drain(phase)
    for stage in range(2):
        sum_drain(stage)
    for copy in halos + pre_halos:
        copy.wait_send()

    tiles = exchange_wait(7)
    for chunk in range(4):
        lanes = pl.ds(chunk * 256, 256)
        value = (total[:, lanes] + mm(tiles, plane[:, lanes], 0, 0)).astype(BF16)
        grad[:, :, lanes] = by_channel_of(value)
    stores.append(pltpu.make_async_copy(grad, grad_out, out_sem.at[2]))
    stores[2].start()

    sum_wait(2)
    stores.append(pltpu.make_async_copy(full_recv, conv_out, out_sem.at[3]))
    stores[3].start()

    exchange_drain(7)
    sum_drain(2)
    for store in stores:
        store.wait()


def deliver(
    act_in, grad_in, mode_in, conv_in, act_out, grad_out, mode_out, conv_out,
    act, grad, packed_mode, packed_conv, mode, conv, in_sem, out_sem,
):
    held = ((act_in, act), (grad_in, grad), (mode_in, packed_mode), (conv_in, packed_conv))
    loads = [pltpu.make_async_copy(*pair, in_sem.at[i]) for i, pair in enumerate(held)]
    kept = ((act, act_out), (grad, grad_out), (mode, mode_out), (conv, conv_out))
    stores = [pltpu.make_async_copy(*pair, out_sem.at[i]) for i, pair in enumerate(kept)]
    for i in (2, 3, 0, 1):
        loads[i].start()
    loads[2].wait()
    for p in range(KZ):
        mode[p] = packed_mode[p][:, :C]
        mode[KZ + p] = packed_mode[p][:, C:]
    stores[2].start()
    loads[3].wait()
    for i in range(9):
        value = packed_conv[2 * i : 2 * i + 2].reshape(64, 128).astype(F32)
        conv[pl.ds(i * 64, 64), :] = value[:, :C]
        conv[pl.ds(576 + i * 64, 64), :] = value[:, C:]
    for r in range(3):
        value = packed_conv[18 + 3 * r : 21 + 3 * r].reshape(96, 128).astype(F32)
        conv[pl.ds(1152 + r * 192, 96), :] = value[:, :C]
        conv[pl.ds(1152 + r * 192 + 96, 96), :] = value[:, C:]
    stores[3].start()
    for i in (0, 1):
        loads[i].wait()
        stores[i].start()
    for store in stores:
        store.wait()


def shards(snapshots, cotangent, mode_weight, conv_weight):
    plane, depth, swap, inside = make_tables()
    any_space = pl.BlockSpec(memory_space=pltpu.HBM)
    vmem = pltpu.VMEM
    dma = pltpu.SemaphoreType.DMA
    outs = pl.pallas_call(
        kernel,
        name="layer",
        out_shape=(
            jax.ShapeDtypeStruct((C, 2, PLANE), BF16),
            jax.ShapeDtypeStruct((C, 2, PLANE), BF16),
            jax.ShapeDtypeStruct((KZ, C, 128), F32),
            jax.ShapeDtypeStruct((32, 32, 128), BF16),
        ),
        in_specs=[any_space] * 8,
        out_specs=(any_space,) * 4,
        scratch_shapes=[
            vmem((C, 2, PLANE), BF16),
            vmem((C, 2, PLANE), BF16),
            vmem((2 * KZ, C, C), BF16),
            vmem((3, 9, C, C), BF16),
            vmem((256, PLANE), BF16),
            vmem((4, 512, 512), BF16),
            vmem((256, 256), BF16),
            vmem((16, PLANE), BF16),
            vmem((C, 2, PLANE), BF16),
            vmem((C, 2, PLANE), BF16),
            vmem((KZ, C, 128), F32),
            vmem((8, G, 16, 128), BF16),
            vmem((8, G, 16, 128), BF16),
            vmem((2, C, PLANE), BF16),
            vmem((2, C, PLANE), BF16),
            vmem((9 * C, 4 * PLANE), BF16),
            vmem((3 * C, 9 * C), BF16),
            vmem((3 * C, 9 * C), BF16),
            vmem((KZ, 128, 128), BF16),
            vmem((KZ, 128, 128), BF16),
            vmem((128, PLANE), F32),
            vmem((128, PLANE), BF16),
            vmem((128, PLANE), BF16),
            vmem((128, PLANE), BF16),
            vmem((128, PLANE), BF16),
            vmem((256, 128), BF16),
            vmem((256, 128), BF16),
            vmem((1024, 128), BF16),
            vmem((32, 32, 128), BF16),
            vmem((32, 128), BF16),
            vmem((8, 32, 128), BF16),
            vmem((32, 128), BF16),
            vmem((32, 32, 128), BF16),
            dma((8,)),
            dma((4,)),
            dma((8,)),
            dma((8,)),
            dma((2, 4)),
            dma((3,)),
            dma((3,)),
        ],
        compiler_params=pltpu.CompilerParams(
            collective_id=0, has_side_effects=True, vmem_limit_bytes=60 << 20
        ),
    )(
        snapshots[0],
        cotangent[0],
        mode_weight.reshape(2 * KZ, C, C),
        conv_weight.reshape(3, 9, C, C),
        jnp.asarray(plane),
        jnp.asarray(depth),
        jnp.asarray(swap),
        jnp.asarray(inside),
    )
    outs = pl.pallas_call(
        deliver,
        name="deliver",
        out_shape=(
            jax.ShapeDtypeStruct((C, 2, PLANE), BF16),
            jax.ShapeDtypeStruct((C, 2, PLANE), BF16),
            jax.ShapeDtypeStruct((2 * KZ, C, C), F32),
            jax.ShapeDtypeStruct((27 * C, C), F32),
        ),
        in_specs=[any_space] * 4,
        out_specs=(any_space,) * 4,
        scratch_shapes=[vmem(out.shape, out.dtype) for out in outs]
        + [vmem((2 * KZ, C, C), F32), vmem((27 * C, C), F32), dma((4,)), dma((4,))],
        compiler_params=pltpu.CompilerParams(vmem_limit_bytes=60 << 20),
    )(*outs)
    activated, input_gradient, mode_gradient, conv_gradient = outs
    return (
        activated.reshape(1, C, 2, PLANE),
        input_gradient.reshape(1, C, 2, PLANE),
        mode_gradient.reshape(1, 1, 2 * KZ, C, C),
        conv_gradient.reshape(3, 3, 3, C, C),
    )


def solution(mesh):
    in_specs = (
        P("batch", None, "space", None),
        P("batch", None, "space", None),
        P("batch", "space", None, None, None),
        P(),
    )
    out_specs = in_specs
    return jax.shard_map(shards, mesh=mesh, in_specs=in_specs, out_specs=out_specs, check_vma=False)
```
